512 devices in a mesh: blk: 512 (over y, z, x, core).
Axes of the slice: x: 4, y: 4, z: 16, core: 2. Of those that a mesh axis runs over, the one named last changes fastest.
Arguments:
- tables: float32 [262144, 400], P('blk'), may hold values from -17 to 17
- state: float32 [262144], P('blk'), may hold values from 1e-05 to 0.001
- relations: float32 [2, 400, 400], replicated, may hold values from -0.3125 to 0.3125
- partner: int32 [2, 512], P(None, 'blk'), may hold values from 0 to 511, as said below
- counts: int32 [2, 512], P(None, 'blk'), may hold values from 1 to 512, as said below
- positive: int32 [2, 262144], P(None, 'blk'), may hold values from 0 to 511
- relation_ids: int32 [2, 262144], P(None, 'blk'), may hold values from 0 to 1
Outputs:
- tables_out: float32 [262144, 400], P('blk')
- state_out: float32 [262144], P('blk')
- relations_out: float32 [2, 400, 400], replicated
- losses: float32 [2], replicated
The draws below stay inside these ranges and needn't reach their ends.
Inputs may be any that keep to these rules, and one draw needn't show every extreme that they name: partner[r, i] = i XOR 2**c_r with one bit number c_r for each round; 512 is a power of two. A block's valid sources in a round are its first counts rows.
All inputs are finite; a program needn't handle non-finite values.
Results may differ from the reference program's by a relative error of at most 0.0078.
Values may be sent and summed in bfloat16 or wider, within the bound.
A program may use at most 64 MiB of HBM per device.

```python
import math
import jax
import jax.numpy as jnp
from jax import lax

D = 400
ROWS = 512
NREL = 2
ROUNDS = 2
BLOCKS = 512
ENTITIES = 262144


def draw_tables(key, part):
    base = jnp.clip(jax.random.normal(key, (BLOCKS * ROWS, D), jnp.float32) * 0.4, -2.4, 2.4)
    return base


def draw_partner(key, part):
    levels = BLOCKS.bit_length() - 1
    picks = jax.random.randint(key, (ROUNDS, 1), 0, levels)
    masks = jnp.left_shift(jnp.ones((ROUNDS, 1), jnp.int32), picks)
    places = jnp.arange(BLOCKS, dtype=jnp.int32)[None, :]
    return jnp.bitwise_xor(places, masks).astype(jnp.int32)


def draw_counts(key, part):
    key_jitter = jax.random.fold_in(key, 11)
    key_size = jax.random.fold_in(key, 23)
    key_sign = jax.random.fold_in(key, 37)
    places = jnp.arange(BLOCKS, dtype=jnp.int32)
    base = ROWS // 4 + places * (ROWS // 2) // BLOCKS
    jitter = jax.random.randint(key_jitter, (ROUNDS, BLOCKS), -(ROWS // 4), ROWS // 4 + 1)
    shift_size = jax.random.randint(key_size, (ROUNDS, 1), ROWS // 8, ROWS // 4 + 1)
    shift_sign = 2 * jax.random.randint(key_sign, (ROUNDS, 1), 0, 2) - 1
    value = jnp.clip(base[None, :] + jitter + shift_sign * shift_size, 1, ROWS)
    return jnp.where(places[None, :] == BLOCKS - 1, ROWS, value).astype(jnp.int32)


def plant(values, own_key, smallest, high):
    extent = values.shape
    spot = [jax.random.randint(jax.random.fold_in(own_key, axis), (), 0, extent[axis]) for axis in range(len(extent))]
    values = values.at[tuple(spot)].set(smallest)
    longest = extent.index(max(extent))
    spot[longest] = (spot[longest] + 1) % extent[longest]
    return values.at[tuple(spot)].set(high)


def steps_of(rng, extent, pieces, least, largest):
    def one(axis_at, shards_of):
        heights = jax.random.uniform(jax.random.fold_in(jax.random.fold_in(rng, 6), axis_at), (shards_of,), jnp.float32, least / len(pieces), largest / len(pieces))
        return jnp.repeat(jnp.exp(heights), extent[axis_at] // shards_of).reshape((-1,) + (1,) * (len(extent) - axis_at - 1))

    gain = one(*pieces[0])
    for cut in pieces[1:]:
        gain = gain * one(*cut)
    return gain


def gaussian(rng, shape, width, reach, kind=jnp.bfloat16):
    array = jax.random.normal(rng, shape, jnp.float32) * width
    return jnp.minimum(jnp.maximum(array, -reach), reach).astype(kind)


def setup_inputs(seed: int = 0) -> dict:
    keys = jax.random.split(jax.random.key(seed), 8)
    return {
        "tables": draw_tables(jax.random.fold_in(keys[7], 71), 0),
        "state": jnp.clip(jnp.exp(math.log(0.001) - 4.6051703 * jax.random.uniform(keys[1], (ENTITIES,), jnp.float32) ** steps_of(keys[1], (ENTITIES,), ((0, 512),), -0.2, 0.2)), 9.999999747378752e-06, 0.001),
        "relations": gaussian(keys[2], (NREL, D, D), D ** -0.5, 0.3125, jnp.float32),
        "partner": draw_partner(jax.random.fold_in(keys[7], 71), 0),
        "counts": draw_counts(jax.random.fold_in(keys[7], 71), 0),
        "positive": plant(jax.random.randint(keys[5], (ROUNDS, ENTITIES), 0, ROWS), jax.random.fold_in(keys[5], 1), 0, ROWS - 1).astype(jnp.int32),
        "relation_ids": plant(jax.random.randint(keys[6], (ROUNDS, ENTITIES), 0, NREL), jax.random.fold_in(keys[6], 1), 0, NREL - 1).astype(jnp.int32),
    }


learn_rate = 0.3
rel_rate = 0.1

def forward(src, dst, rel_ids, pos, count, relb, weight):
    rows = src.shape[0]
    kinds = jnp.arange(relb.shape[0], dtype=jnp.int32)
    choose = (rel_ids[:, None] == kinds[None, :]).astype(jnp.float32)
    query = jnp.zeros((rows, src.shape[1]), jnp.float32)
    for kind in range(relb.shape[0]):
        query = query + choose[:, kind:kind + 1] * jnp.dot(src, relb[kind], preferred_element_type=jnp.float32)
    query_b = query.astype(jnp.bfloat16)
    scores = lax.dot_general(query_b, dst, (((1,), (1,)), ((), ())), preferred_element_type=jnp.float32)
    top = lax.optimization_barrier(jnp.max(scores, axis=1, keepdims=True))
    shifted = jnp.exp(scores - top)
    denom = lax.optimization_barrier(jnp.sum(shifted, axis=1, keepdims=True))
    columns = jnp.arange(dst.shape[0], dtype=jnp.int32)
    target = (pos[:, None] == columns[None, :]).astype(jnp.float32)
    valid = (jnp.arange(rows, dtype=jnp.int32) < count).astype(jnp.float32)
    per_row = jnp.log(denom[:, 0]) + top[:, 0] - lax.optimization_barrier(jnp.sum(scores * target, axis=1))
    loss_part = jnp.sum(valid * per_row)
    slope = (weight * valid[:, None] * (shifted / denom - target)).astype(jnp.bfloat16)
    return (loss_part, slope, query_b, choose)

def backward_source(src, dst, slope, choose, relb):
    dquery = jnp.dot(slope, dst, preferred_element_type=jnp.float32).astype(jnp.bfloat16)
    grad_src = jnp.zeros(src.shape, jnp.float32)
    grads = []
    for kind in range(relb.shape[0]):
        part = lax.dot_general(dquery, relb[kind], (((1,), (1,)), ((), ())), preferred_element_type=jnp.float32)
        grad_src = grad_src + choose[:, kind:kind + 1] * part
        picked = src * choose[:, kind:kind + 1].astype(jnp.bfloat16)
        grads.append(lax.dot_general(picked, dquery, (((0,), (0,)), ((), ())), preferred_element_type=jnp.float32))
    return (grad_src, jnp.stack(grads))

def grad_dest(slope, query_b):
    return lax.dot_general(slope, query_b, (((0,), (0,)), ((), ())), preferred_element_type=jnp.float32).astype(jnp.bfloat16)

def reference(tables, state, relations, partner, counts, positive, relation_ids):
    blocks = tables.reshape(BLOCKS, ROWS, D)
    accum = state.reshape(BLOCKS, ROWS)
    relb = relations.astype(jnp.bfloat16)
    rel_grad = jnp.zeros(relations.shape, jnp.float32)
    losses = []
    for rnd in range(ROUNDS):
        totals = jnp.sum(counts[rnd].astype(jnp.float32))
        weight = BLOCKS / totals
        table_b = blocks.astype(jnp.bfloat16)
        dests = table_b[partner[rnd]]
        pos = positive[rnd].reshape(BLOCKS, ROWS)
        rid = relation_ids[rnd].reshape(BLOCKS, ROWS)

        def visit(carry, item):
            src, dst, ids, rows_pos, count = item
            loss_part, slope, query_b, choose = forward(src, dst, ids, rows_pos, count, relb, weight)
            grad_src, grads = backward_source(src, dst, slope, choose, relb)
            return (carry + grads, (loss_part, grad_src, grad_dest(slope, query_b)))
        rel_grad, (loss_parts, grad_srcs, grad_dsts) = lax.scan(visit, rel_grad, (table_b, dests, rid, pos, counts[rnd]))
        grad = grad_srcs + grad_dsts[partner[rnd]].astype(jnp.float32)
        accum = accum + lax.optimization_barrier(jnp.mean(grad * grad, axis=2))
        blocks = blocks - learn_rate * grad / jnp.sqrt(accum)[:, :, None]
        losses.append(jnp.sum(loss_parts) / totals)
    relations_out = relations - rel_rate * rel_grad
    return (blocks.reshape(ENTITIES, D), accum.reshape(ENTITIES), relations_out, jnp.stack(losses))
```

```python
import functools

import jax
import jax.numpy as jnp
from jax import lax
from jax.experimental import pallas as pl
from jax.experimental.pallas import tpu as pltpu
from jax.sharding import PartitionSpec as P

ROUNDS = 2
LEARN_RATE = 0.3
REL_RATE = 0.1
MESH = pl.DeviceIdType.MESH

NY, NZ, NX = 4, 16, 4
PLANE = NY * NX
LANES = 128
TILES = 80
SHARE = TILES // PLANE
OWNERS = SHARE * 2

VMEM = pl.BlockSpec(memory_space=pltpu.VMEM)
ANY = pl.BlockSpec(memory_space=pl.ANY)


def dot_nn(a, b):
    return lax.dot_general(a, b, (((1,), (0,)), ((), ())), preferred_element_type=jnp.float32)


def dot_nt(a, b):
    return lax.dot_general(a, b, (((1,), (1,)), ((), ())), preferred_element_type=jnp.float32)


def eye(n):
    rows = lax.broadcasted_iota(jnp.int32, (n, n), 0)
    return (rows == lax.broadcasted_iota(jnp.int32, (n, n), 1)).astype(jnp.bfloat16)


def coords():
    me = lax.axis_index("blk")
    core = me % 2
    x = (me // 2) % NX
    z = (me // (2 * NX)) % NZ
    y = me // (2 * NX * NZ)
    return y, z, x, core


def index_of(y, z, x, core):
    return ((y * NZ + z) * NX + x) * 2 + core


def prep_kernel(tables, relations, positive, relation_ids, counts, et, ebt, rb, rbt, meta, cnt):
    table_t = tables[...].T
    et[...] = table_t
    ebt[...] = table_t.astype(jnp.bfloat16)
    ident = eye(rb.shape[1])
    for kind in range(rb.shape[0]):
        op = relations[kind].astype(jnp.bfloat16)
        rb[kind] = op
        rbt[kind] = dot_nt(ident, op).astype(jnp.bfloat16)
    meta[0:2, :] = positive[...]
    meta[2:4, :] = relation_ids[...]
    wide = jnp.broadcast_to(counts[...], (ROUNDS, meta.shape[1]))
    meta[4:6, :] = wide
    meta[6:8, :] = wide
    cnt[...] = jnp.zeros(cnt.shape, jnp.float32)
    cnt[0:2, :] = jnp.broadcast_to(counts[...].astype(jnp.float32), (ROUNDS, LANES))


def pair_of(bit):
    me = lax.axis_index("blk")
    step = 1 << bit
    return me + step * (1 - 2 * ((me // step) % 2))


def plane_peer(d):
    y, z, x, core = coords()
    return index_of((y + (d // (2 * NX))) % NY, z, (x + (d // 2) % NX) % NX, (core + d % 2) % 2)


def line_peer(d):
    y, z, x, core = coords()
    return index_of(y, (z + d) % NZ, x, core)


def exchange_first(bit, ebt, meta, cnt, ept, metap, tot,
                   part, aslot, bslot, sems, asend, arecv, bsend, brecv):
    partner = pair_of(bit)
    barrier = pltpu.get_barrier_semaphore()

    def greet(peer):
        pl.semaphore_signal(barrier, inc=1, device_id=(peer,), device_id_type=MESH)

    greet(partner)

    @pl.loop(1, 2 * PLANE)
    def _(d):
        greet(plane_peer(d))

    @pl.loop(1, NZ)
    def _(d):
        greet(line_peer(d))

    pl.semaphore_wait(barrier, 1 + (2 * PLANE - 1) + (NZ - 1))

    def acopy(d):
        return pltpu.make_async_remote_copy(
            cnt, aslot.at[d - 1], asend.at[d - 1], arecv.at[d - 1],
            device_id=(plane_peer(d),), device_id_type=MESH)

    def bcopy(d):
        return pltpu.make_async_remote_copy(
            part, bslot.at[d - 1], bsend.at[d - 1], brecv.at[d - 1],
            device_id=(line_peer(d),), device_id_type=MESH)

    @pl.loop(1, 2 * PLANE)
    def _(d):
        acopy(d).start()

    block = pltpu.make_async_remote_copy(
        ebt, ept, sems.at[0], sems.at[1], device_id=(partner,), device_id_type=MESH)
    small = pltpu.make_async_remote_copy(
        meta, metap, sems.at[2], sems.at[3], device_id=(partner,), device_id_type=MESH)
    small.start()
    block.start()

    @pl.loop(1, 2 * PLANE)
    def _(d):
        acopy(d).wait()

    part[...] = cnt[...] + jnp.sum(aslot[...], axis=0)

    @pl.loop(1, NZ)
    def _(d):
        bcopy(d).start()

    @pl.loop(1, NZ)
    def _(d):
        bcopy(d).wait()

    tot[...] = part[...] + jnp.sum(bslot[...], axis=0)
    small.wait()
    block.wait()


def exchange_next(bit, ebt, meta, ept, metap, sems):
    partner = pair_of(bit)
    barrier = pltpu.get_barrier_semaphore()
    pl.semaphore_signal(barrier, inc=1, device_id=(partner,), device_id_type=MESH)
    pl.semaphore_wait(barrier, 1)
    block = pltpu.make_async_remote_copy(
        ebt, ept, sems.at[0], sems.at[1], device_id=(partner,), device_id_type=MESH)
    small = pltpu.make_async_remote_copy(
        meta, metap, sems.at[2], sems.at[3], device_id=(partner,), device_id_type=MESH)
    small.start()
    block.start()
    small.wait()
    block.wait()


def pick(ids, parts):
    out = parts[0]
    for kind in range(1, len(parts)):
        out = jnp.where(ids == kind, parts[kind], out)
    return out


def bucket(dst, query_t, pos, count, weight):
    scores = dot_nn(dst, query_t)
    top = jnp.max(scores, axis=0, keepdims=True)
    shifted = jnp.exp(scores - top)
    denom = jnp.sum(shifted, axis=0, keepdims=True)
    hit = lax.broadcasted_iota(jnp.int32, scores.shape, 0) == pos
    aim = jnp.sum(jnp.where(hit, scores, 0.0), axis=0, keepdims=True)
    valid = lax.broadcasted_iota(jnp.int32, pos.shape, 1) < count
    scale = jnp.where(valid, weight, 0.0)
    slope = scale * (shifted * (1.0 / denom) - jnp.where(hit, 1.0, 0.0))
    rows = jnp.where(valid, jnp.log(denom) + top - aim, 0.0)
    return slope.astype(jnp.bfloat16), rows


def round_kernel(rnd, last, blocks, et, ebt, ept, meta, metap, tot, state, rb, rbt, *refs):
    if last:
        qin, lin, tables_out, state_out, qout, lout = refs
    else:
        et_out, ebt_out, state_out, qout, lout = refs
    kinds = rb.shape[0]
    width = rb.shape[1]
    rows = ebt.shape[1]
    own_t = ebt[...]
    far_t = ept[...]
    ident = eye(rows)
    own = dot_nt(ident, own_t).astype(jnp.bfloat16)
    far = dot_nt(ident, far_t).astype(jnp.bfloat16)
    weight = blocks / tot[rnd : rnd + 1, 0:1]
    pos, ids, count = meta[rnd : rnd + 1, :], meta[2 + rnd : 3 + rnd, :], meta[4 + rnd : 5 + rnd, :]
    pos_p, ids_p = metap[rnd : rnd + 1, :], metap[2 + rnd : 3 + rnd, :]
    count_p = metap[4 + rnd : 5 + rnd, :]

    query = pick(ids, [dot_nn(rbt[k], own_t) for k in range(kinds)]).astype(jnp.bfloat16)
    query_p = pick(ids_p, [dot_nn(rbt[k], far_t) for k in range(kinds)]).astype(jnp.bfloat16)
    slope_p, _ = bucket(own, query_p, pos_p, count_p, weight)
    slope, loss = bucket(far, query, pos, count, weight)
    dq = dot_nn(far_t, slope).astype(jnp.bfloat16)
    grad = pick(ids, [dot_nn(rb[k], dq) for k in range(kinds)])
    grad = grad + dot_nt(query_p, slope_p).astype(jnp.bfloat16).astype(jnp.float32)
    acc = state[...] + jnp.mean(grad * grad, axis=0, keepdims=True)
    state_out[...] = acc
    fresh = et[...] - LEARN_RATE * grad / jnp.sqrt(acc)
    if last:
        tables_out[...] = fresh.T
    else:
        et_out[...] = fresh
        ebt_out[...] = fresh.astype(jnp.bfloat16)

    full = width // LANES
    tall = width // 16
    edge = full * LANES
    for kind in range(kinds):
        picked = jnp.where(ids == kind, own_t, jnp.zeros_like(own_t))
        main = dot_nt(picked, dq)
        side = dot_nt(dq[edge:, :], picked)
        side = jnp.concatenate([side, jnp.zeros((16, 4 * LANES - width), jnp.float32)], axis=1)
        for j in range(full):
            piece = main[:, j * LANES : (j + 1) * LANES].reshape(tall, 16, LANES)
            if last:
                piece = piece + qin[kind, j * tall : (j + 1) * tall]
            qout[kind, j * tall : (j + 1) * tall] = piece
        for j in range(4):
            piece = side[:, j * LANES : (j + 1) * LANES]
            if last:
                piece = piece + qin[kind, full * tall + j]
            qout[kind, full * tall + j] = piece
    total = jnp.sum(loss, axis=1, keepdims=True)
    lane = lax.broadcasted_iota(jnp.int32, (16, LANES), 1)
    row = lax.broadcasted_iota(jnp.int32, (16, LANES), 0)
    mark = jnp.where((lane == rnd) & (row == 0), jnp.broadcast_to(total, (16, LANES)), 0.0)
    if last:
        mark = mark + lin[...]
    lout[...] = mark
    qout[0, TILES - 1] = mark
    for kind in range(1, kinds):
        qout[kind, TILES - 1] = jnp.zeros((16, LANES), jnp.float32)


def reduce_kernel(q, relations, tot, rel_out, loss_out,
                  csend, crecv, acc, xsend, xslot, zpart, zslot, zres, fin, sib,
                  s_core, s_xs, s_xr, s_zs, s_zr, s_gs, s_gr, s_as, s_ar, s_bs, s_br):
    y, z, x, core = coords()
    plane = y * NX + x
    other = 1 - core
    twin = index_of(y, z, x, other)

    def near(d):
        return index_of((y + d // NX) % NY, z, (x + d % NX) % NX, core)

    def near_plane(d):
        return ((y + d // NX) % NY) * NX + (x + d % NX) % NX

    def from_plane(d):
        return ((y + NY - d // NX) % NY) * NX + (x + NX - d % NX) % NX

    barrier = pltpu.get_barrier_semaphore()

    def greet(peer):
        pl.semaphore_signal(barrier, inc=1, device_id=(peer,), device_id_type=MESH)

    greet(twin)

    @pl.loop(1, PLANE)
    def _(d):
        greet(near(d))

    @pl.loop(1, NZ)
    def _(d):
        greet(line_peer(d))

    csend[...] = q[other].astype(jnp.bfloat16)
    pl.semaphore_wait(barrier, 1 + (PLANE - 1) + (NZ - 1))

    swap = pltpu.make_async_remote_copy(
        csend, crecv, s_core.at[0], s_core.at[1], device_id=(twin,), device_id_type=MESH)
    swap.start()
    swap.wait()
    both = q[core] + crecv[...].astype(jnp.float32)
    acc[...] = both.reshape(PLANE, SHARE, 16, LANES)
    xsend[...] = both.astype(jnp.bfloat16).reshape(PLANE, SHARE, 16, LANES)

    def xcopy(d):
        return pltpu.make_async_remote_copy(
            xsend.at[near_plane(d)], xslot.at[d - 1], s_xs.at[d - 1], s_xr.at[d - 1],
            device_id=(near(d),), device_id_type=MESH)

    @pl.loop(1, PLANE)
    def _(d):
        xcopy(d).start()

    @pl.loop(1, PLANE)
    def _(d):
        xcopy(d).wait()

    part = acc[plane]
    for d in range(PLANE - 1):
        part = part + xslot[d].astype(jnp.float32)
    zpart[...] = part.reshape(OWNERS, 8, LANES)

    def zcopy(d):
        return pltpu.make_async_remote_copy(
            zpart.at[(z + d) % NZ], zslot.at[d - 1], s_zs.at[d - 1], s_zr.at[d - 1],
            device_id=(line_peer(d),), device_id_type=MESH)

    @pl.loop(1, NZ)
    def _(d):
        @pl.when((z + d) % NZ < OWNERS)
        def _():
            zcopy(d).start()

    def gcopy(d, owner):
        return pltpu.make_async_remote_copy(
            zres.at[owner], zres.at[owner], s_gs.at[d - 1], s_gr.at[owner],
            device_id=(line_peer(d),), device_id_type=MESH)

    @pl.when(z < OWNERS)
    def _():
        @pl.loop(1, NZ)
        def _(d):
            pltpu.make_async_remote_copy(
                zpart.at[0], zslot.at[d - 1], s_zs.at[d - 1], s_zr.at[d - 1],
                device_id=(line_peer(d),), device_id_type=MESH).wait_recv()

        total = zpart[z]
        for d in range(NZ - 1):
            total = total + zslot[d]
        zres[z] = total

        @pl.loop(1, NZ)
        def _(d):
            gcopy(d, z).start()

    @pl.loop(1, NZ)
    def _(d):
        @pl.when((z + d) % NZ < OWNERS)
        def _():
            zcopy(d).wait_send()

    @pl.loop(0, OWNERS)
    def _(o):
        @pl.when(o != z)
        def _():
            gcopy(1, o).wait_recv()

    whole = zres[...].reshape(SHARE, 16, LANES)
    tail = whole[SHARE - 1]
    rest = tail[0:8] - tail[0:8].astype(jnp.bfloat16).astype(jnp.float32)
    tail = jnp.concatenate([tail[0:8], jnp.where(plane == PLANE - 1, rest, tail[8:16])], axis=0)
    fin[plane] = whole.astype(jnp.bfloat16)
    fin[plane, SHARE - 1] = tail.astype(jnp.bfloat16)

    def ncopy(d):
        return pltpu.make_async_remote_copy(
            fin.at[plane], fin.at[plane], s_as.at[d - 1], s_ar.at[d - 1],
            device_id=(near(d),), device_id_type=MESH)

    def tcopy(piece, slot):
        return pltpu.make_async_remote_copy(
            fin.at[piece], sib.at[piece], s_bs.at[slot], s_br.at[slot],
            device_id=(twin,), device_id_type=MESH)

    @pl.loop(1, PLANE)
    def _(d):
        ncopy(d).start()

    tcopy(plane, 0).start()

    @pl.when(z < OWNERS)
    def _():
        @pl.loop(1, NZ)
        def _(d):
            gcopy(d, z).wait_send()

    @pl.loop(1, PLANE)
    def _(d):
        pltpu.make_async_remote_copy(
            fin.at[from_plane(d)], fin.at[from_plane(d)], s_as.at[d - 1], s_ar.at[d - 1],
            device_id=(near(d),), device_id_type=MESH).wait_recv()
        tcopy(from_plane(d), d).start()

    width = relations.shape[1]
    full = width // LANES
    tall = width // 16
    edge = full * LANES

    def finish(kind, ref):
        summed = ref[...].reshape(TILES, 16, LANES).astype(jnp.float32)
        for j in range(full):
            piece = summed[j * tall : (j + 1) * tall].reshape(width, LANES)
            span = slice(j * LANES, (j + 1) * LANES)
            rel_out[kind, :, span] = relations[kind, :, span] - REL_RATE * piece
        side = jnp.concatenate([summed[full * tall + j] for j in range(4)], axis=1)
        rel_out[kind, :, edge:] = relations[kind, :, edge:] - REL_RATE * side.T[:width, :]

    finish(core, fin)

    @pl.loop(0, PLANE)
    def _(d):
        tcopy(from_plane(d), d).wait()

    @pl.loop(1, PLANE)
    def _(d):
        ncopy(d).wait_send()

    finish(other, sib)

    def loss_of(ref):
        tile = ref[PLANE - 1, SHARE - 1].astype(jnp.float32)
        return tile[0:8] + tile[8:16]

    @pl.when(core == 0)
    def _():
        loss_out[...] = loss_of(fin)

    @pl.when(core == 1)
    def _():
        loss_out[...] = loss_of(sib)


def on_device(tables, state, relations, partner, counts, positive, relation_ids):
    rows, width = tables.shape
    kinds = relations.shape[0]
    blocks = lax.axis_size("blk")
    depth = blocks.bit_length() - 1
    me = lax.axis_index("blk")
    f32, bf16, i32 = jnp.float32, jnp.bfloat16, jnp.int32
    shape = jax.ShapeDtypeStruct
    DMA = pltpu.SemaphoreType.DMA

    offset = jnp.bitwise_xor(partner[:, 0], me)
    level = jnp.zeros((ROUNDS,), i32)
    for bit in range(1, depth):
        level = level + (offset >> bit > 0).astype(i32)

    et, ebt, rb, rbt, meta, cnt = pl.pallas_call(
        prep_kernel,
        out_shape=(
            shape((width, rows), f32), shape((width, rows), bf16),
            shape(relations.shape, bf16), shape(relations.shape, bf16),
            shape((8, rows), i32), shape((8, LANES), f32),
        ),
        in_specs=[VMEM] * 5,
        out_specs=(VMEM,) * 6,
        name="prep",
    )(tables, relations, positive, relation_ids, counts)

    def first(bit, ebt, meta, cnt):
        return pl.pallas_call(
            functools.partial(exchange_first, bit),
            out_shape=(shape(ebt.shape, bf16), shape(meta.shape, i32), shape(cnt.shape, f32)),
            in_specs=[ANY, ANY, VMEM],
            out_specs=(ANY, ANY, VMEM),
            scratch_shapes=[
                pltpu.VMEM((8, LANES), f32),
                pltpu.VMEM((2 * PLANE - 1, 8, LANES), f32),
                pltpu.VMEM((NZ - 1, 8, LANES), f32),
                DMA((4,)),
                DMA((2 * PLANE - 1,)), DMA((2 * PLANE - 1,)),
                DMA((NZ - 1,)), DMA((NZ - 1,)),
            ],
            compiler_params=pltpu.CompilerParams(collective_id=bit, has_side_effects=True),
            name="swap_a",
        )(ebt, meta, cnt)

    def following(bit, ebt, meta):
        return pl.pallas_call(
            functools.partial(exchange_next, bit),
            out_shape=(shape(ebt.shape, bf16), shape(meta.shape, i32)),
            in_specs=[ANY, ANY],
            out_specs=(ANY, ANY),
            scratch_shapes=[DMA((4,))],
            compiler_params=pltpu.CompilerParams(collective_id=depth + bit, has_side_effects=True),
            name="swap_b",
        )(ebt, meta)

    qshape = shape((kinds, TILES, 16, LANES), f32)
    lshape = shape((16, LANES), f32)
    accum = state.reshape(1, rows)

    ept, metap, tot = lax.switch(
        level[0], [functools.partial(first, bit) for bit in range(depth)], ebt, meta, cnt)
    et, ebt2, accum, q, loss = pl.pallas_call(
        functools.partial(round_kernel, 0, False, float(blocks)),
        out_shape=(shape((width, rows), f32), shape((width, rows), bf16),
                   shape((1, rows), f32), qshape, lshape),
        in_specs=[VMEM] * 9,
        out_specs=(VMEM,) * 5,
        name="round_a",
    )(et, ebt, ept, meta, metap, tot, accum, rb, rbt)

    ept, metap = lax.switch(
        level[1], [functools.partial(following, bit) for bit in range(depth)], ebt2, meta)
    tables_out, accum, q, loss = pl.pallas_call(
        functools.partial(round_kernel, 1, True, float(blocks)),
        out_shape=(shape((rows, width), f32), shape((1, rows), f32), qshape, lshape),
        in_specs=[VMEM] * 11,
        out_specs=(VMEM,) * 4,
        name="round_b",
    )(et, ebt2, ept, meta, metap, tot, accum, rb, rbt, q, loss)

    relations_out, sums = pl.pallas_call(
        reduce_kernel,
        out_shape=(shape(relations.shape, f32), shape((8, LANES), f32)),
        in_specs=[VMEM] * 3,
        out_specs=(VMEM,) * 2,
        scratch_shapes=[
            pltpu.VMEM((TILES, 16, LANES), bf16),
            pltpu.VMEM((TILES, 16, LANES), bf16),
            pltpu.VMEM((PLANE, SHARE, 16, LANES), f32),
            pltpu.VMEM((PLANE, SHARE, 16, LANES), bf16),
            pltpu.VMEM((PLANE - 1, SHARE, 16, LANES), bf16),
            pltpu.VMEM((OWNERS, 8, LANES), f32),
            pltpu.VMEM((NZ - 1, 8, LANES), f32),
            pltpu.VMEM((OWNERS, 8, LANES), f32),
            pltpu.VMEM((PLANE, SHARE, 16, LANES), bf16),
            pltpu.VMEM((PLANE, SHARE, 16, LANES), bf16),
            DMA((2,)),
            DMA((PLANE - 1,)), DMA((PLANE - 1,)),
            DMA((NZ - 1,)), DMA((NZ - 1,)),
            DMA((NZ - 1,)), DMA((OWNERS,)),
            DMA((PLANE - 1,)), DMA((PLANE - 1,)),
            DMA((PLANE,)), DMA((PLANE,)),
        ],
        compiler_params=pltpu.CompilerParams(collective_id=2 * depth, has_side_effects=True),
        name="reduce",
    )(q, relations, tot)

    losses = sums[0, :ROUNDS] / tot[:ROUNDS, 0]
    return (tables_out, accum.reshape(rows), relations_out, losses)


def solution(mesh):
    return jax.shard_map(
        on_device,
        mesh=mesh,
        in_specs=(
            P("blk", None),
            P("blk"),
            P(),
            P(None, "blk"),
            P(None, "blk"),
            P(None, "blk"),
            P(None, "blk"),
        ),
        out_specs=(P("blk", None), P("blk"), P(), P()),
        check_vma=False,
    )
```

```python
import functools

import jax
import jax.numpy as jnp
from jax import lax
from jax.experimental import pallas as pl
from jax.experimental.pallas import tpu as pltpu
from jax.sharding import PartitionSpec as P

ROUNDS = 2
LEARN_RATE = 0.3
REL_RATE = 0.1
MESH = pl.DeviceIdType.MESH

NY, NZ, NX = 4, 16, 4
PLANE = NY * NX
LANES = 128
TILES = 80
SHARE = TILES // PLANE
OWNERS = SHARE * 2

VMEM = pl.BlockSpec(memory_space=pltpu.VMEM)
ANY = pl.BlockSpec(memory_space=pl.ANY)


def dot_nn(a, b):
    return lax.dot_general(a, b, (((1,), (0,)), ((), ())), preferred_element_type=jnp.float32)


def dot_nt(a, b):
    return lax.dot_general(a, b, (((1,), (1,)), ((), ())), preferred_element_type=jnp.float32)


def eye(n):
    rows = lax.broadcasted_iota(jnp.int32, (n, n), 0)
    return (rows == lax.broadcasted_iota(jnp.int32, (n, n), 1)).astype(jnp.bfloat16)


def coords():
    me = lax.axis_index("blk")
    core = lax.rem(me, 2)
    x = lax.rem(lax.div(me, 2), NX)
    z = lax.rem(lax.div(me, 2 * NX), NZ)
    y = lax.div(me, 2 * NX * NZ)
    return y, z, x, core


def spots():
    y, z, x, core = coords()
    ys = [lax.rem(y + d, NY) for d in range(NY)]
    zs = [lax.rem(z + d, NZ) for d in range(NZ)]
    xs = [lax.rem(x + d, NX) for d in range(NX)]
    return ys, zs, xs, core


def index_of(y, z, x, core):
    return y * (2 * NX * NZ) + z * (2 * NX) + x * 2 + core


def hops(d, size):
    return min(d, size - d)


PLANE_STEPS = sorted(
    [(dy, dx) for dy in range(NY) for dx in range(NX) if dy or dx],
    key=lambda s: -(hops(s[0], NY) + hops(s[1], NX)))
LINE_STEPS = sorted(range(1, NZ), key=lambda d: -hops(d, NZ))


def greet(peer):
    pl.semaphore_signal(
        pltpu.get_barrier_semaphore(), inc=1, device_id=(peer,), device_id_type=MESH)


def send(src, dst, send_sem, recv_sem, peer):
    return pltpu.make_async_remote_copy(
        src, dst, send_sem, recv_sem, device_id=(peer,), device_id_type=MESH)


def pair_of(bit):
    me = lax.axis_index("blk")
    step = 1 << bit
    return me + step * (1 - 2 * lax.rem(lax.div(me, step), 2))


def own_forms(ebt, rbt, ids, own, query):
    own_t = ebt[...]
    own[...] = dot_nt(eye(own_t.shape[1]), own_t).astype(jnp.bfloat16)
    parts = [dot_nn(rbt[k], own_t) for k in range(rbt.shape[0])]
    query[...] = pick(ids, parts).astype(jnp.bfloat16)


def exchange_first(bit, et, relations, positive, relation_ids, counts,
                   ebt, rb, rbt, meta, ept, metap, tot, own, query,
                   et_v, rel_v, cnt, part, aslot, bslot, loads, sems, asend, arecv, bsend, brecv):
    ys, zs, xs, core = spots()
    partner = pair_of(bit)
    load_e = pltpu.make_async_copy(et, et_v, loads.at[0])
    load_r = pltpu.make_async_copy(relations, rel_v, loads.at[1])
    load_e.start()
    load_r.start()

    near = [index_of(ys[dy], zs[0], xs[dx], core) for dy, dx in PLANE_STEPS]
    near += [index_of(ys[dy], zs[0], xs[dx], 1 - core) for dy, dx in PLANE_STEPS]
    near += [index_of(ys[0], zs[0], xs[0], 1 - core)]
    line = [index_of(ys[0], zs[d], xs[0], core) for d in LINE_STEPS]
    for peer in line + near + [partner]:
        greet(peer)

    meta[0:2, :] = positive[...]
    meta[2:4, :] = relation_ids[...]
    cnt[...] = jnp.zeros(cnt.shape, jnp.float32)
    for rnd in range(ROUNDS):
        one = counts[0:1, rnd : rnd + 1]
        meta[4 + rnd : 5 + rnd, :] = jnp.broadcast_to(one, (1, meta.shape[1]))
        meta[6 + rnd : 7 + rnd, :] = jnp.broadcast_to(one, (1, meta.shape[1]))
        cnt[rnd : rnd + 1, :] = jnp.broadcast_to(one.astype(jnp.float32), (1, LANES))
    load_e.wait()
    ebt[...] = et_v[...].astype(jnp.bfloat16)
    pl.semaphore_wait(pltpu.get_barrier_semaphore(), len(line) + len(near) + 1)

    acopies = [send(cnt, aslot.at[i], asend.at[i], arecv.at[i], peer) for i, peer in enumerate(near)]
    bcopies = [send(part, bslot.at[i], bsend.at[i], brecv.at[i], peer) for i, peer in enumerate(line)]
    small = send(meta, metap, sems.at[2], sems.at[3], partner)
    block = send(ebt, ept, sems.at[0], sems.at[1], partner)
    for c in acopies:
        c.start()
    small.start()
    block.start()

    load_r.wait()
    ident = eye(rb.shape[1])
    for kind in range(rb.shape[0]):
        op = rel_v[kind].astype(jnp.bfloat16)
        rb[kind] = op
        rbt[kind] = dot_nt(ident, op).astype(jnp.bfloat16)

    for c in acopies:
        c.wait()
    part[...] = cnt[...] + jnp.sum(aslot[...], axis=0)
    for c in bcopies:
        c.start()
    own_forms(ebt, rbt, meta[2:3, :], own, query)
    for c in bcopies:
        c.wait()
    tot[...] = part[...] + jnp.sum(bslot[...], axis=0)
    small.wait()
    block.wait()


def exchange_next(bit, ebt, meta, rbt, ept, metap, own, query, sems):
    partner = pair_of(bit)
    greet(partner)
    pl.semaphore_wait(pltpu.get_barrier_semaphore(), 1)
    small = send(meta, metap, sems.at[2], sems.at[3], partner)
    block = send(ebt, ept, sems.at[0], sems.at[1], partner)
    small.start()
    block.start()
    own_forms(ebt, rbt, meta[3:4, :], own, query)
    small.wait()
    block.wait()


def pick(ids, parts):
    out = parts[0]
    for kind in range(1, len(parts)):
        out = jnp.where(ids == kind, parts[kind], out)
    return out


def bucket(dst, query_t, pos, count, weight):
    scores = dot_nn(dst, query_t)
    top = jnp.max(scores, axis=0, keepdims=True)
    shifted = jnp.exp(scores - top)
    denom = jnp.sum(shifted, axis=0, keepdims=True)
    hit = lax.broadcasted_iota(jnp.int32, scores.shape, 0) == pos
    aim = jnp.sum(jnp.where(hit, scores, 0.0), axis=0, keepdims=True)
    valid = lax.broadcasted_iota(jnp.int32, pos.shape, 1) < count
    scale = jnp.where(valid, weight, 0.0)
    slope = scale * (shifted * (1.0 / denom) - jnp.where(hit, 1.0, 0.0))
    rows = jnp.where(valid, jnp.log(denom) + top - aim, 0.0)
    return slope.astype(jnp.bfloat16), rows


def relation_part(kind, rounds, mark, out):
    width = rounds[0][0].shape[0]
    full, tall = width // LANES, width // 16
    main = side = 0.0
    for own_t, dq, ids in rounds:
        picked = jnp.where(ids == kind, own_t, jnp.zeros_like(own_t))
        main = main + dot_nt(picked, dq)
        side = side + dot_nt(dq[full * LANES :, :], picked)
    side = jnp.concatenate([side, jnp.zeros((16, 4 * LANES - width), jnp.float32)], axis=1)
    for j in range(full):
        out[j * tall : (j + 1) * tall] = main[:, j * LANES : (j + 1) * LANES].reshape(tall, 16, LANES)
    for j in range(4):
        out[full * tall + j] = side[:, j * LANES : (j + 1) * LANES]
    out[TILES - 1] = jnp.where(kind == 0, mark, 0.0)


def loss_mark(loss, rnd):
    total = jnp.sum(loss, axis=1, keepdims=True)
    lane = lax.broadcasted_iota(jnp.int32, (16, LANES), 1)
    row = lax.broadcasted_iota(jnp.int32, (16, LANES), 0)
    return jnp.where((lane == rnd) & (row == 0), jnp.broadcast_to(total, (16, LANES)), 0.0)


def gradients(rnd, blocks, ept, own, query, meta, metap, tot, rb, rbt, then):
    kinds = rb.shape[0]
    far_t = ept[...]
    far = dot_nt(eye(far_t.shape[1]), far_t).astype(jnp.bfloat16)
    weight = blocks / tot[rnd : rnd + 1, 0:1]
    pos, ids, count = meta[rnd : rnd + 1, :], meta[2 + rnd : 3 + rnd, :], meta[4 + rnd : 5 + rnd, :]
    pos_p, ids_p = metap[rnd : rnd + 1, :], metap[2 + rnd : 3 + rnd, :]
    count_p = metap[4 + rnd : 5 + rnd, :]

    slope, loss = bucket(far, query[...], pos, count, weight)
    dq = dot_nn(far_t, slope).astype(jnp.bfloat16)
    then(ids, dq, loss_mark(loss, rnd))
    query_p = pick(ids_p, [dot_nn(rbt[k], far_t) for k in range(kinds)]).astype(jnp.bfloat16)
    slope_p, _ = bucket(own[...], query_p, pos_p, count_p, weight)
    grad = pick(ids, [dot_nn(rb[k], dq) for k in range(kinds)])
    return grad + dot_nt(query_p, slope_p).astype(jnp.bfloat16).astype(jnp.float32)


def adagrad(et, state, grad):
    acc = state + jnp.mean(grad * grad, axis=0, keepdims=True)
    return acc, et - LEARN_RATE * grad / jnp.sqrt(acc)


def round_kernel(blocks, et, ept, own, query, meta, metap, tot, state, rb, rbt,
                 et_out, ebt_out, state_out, dq_out, mark_out, et_v, loads):
    load_e = pltpu.make_async_copy(et, et_v, loads.at[0])
    load_e.start()

    def keep(ids, dq, mark):
        dq_out[...] = dq
        mark_out[...] = mark

    grad = gradients(0, blocks, ept, own, query, meta, metap, tot, rb, rbt, keep)
    load_e.wait()
    acc, fresh = adagrad(et_v[...], state[...], grad)
    state_out[...] = acc
    et_out[...] = fresh
    ebt_out[...] = fresh.astype(jnp.bfloat16)


def last_kernel(blocks, et, ebt, ept, own, query, meta, metap, tot, state, rb, rbt, ebt_a, dq_a, mark_a, relations,
                et_out, state_out, rel_out, loss_out,
                rel_v, grad_v, csend, crecv, acc, xsend, xslot, zpart, zslot, zres, fin, sib,
                loads, s_core, s_xs, s_xr, s_zs, s_zr, s_gs, s_gr, s_as, s_ar, s_bs, s_br):
    ys, zs, xs, core = spots()
    back_y = [lax.rem(ys[0] + NY - d, NY) for d in range(NY)]
    back_x = [lax.rem(xs[0] + NX - d, NX) for d in range(NX)]
    z = zs[0]
    plane = ys[0] * NX + xs[0]
    other = 1 - core
    twin = index_of(ys[0], z, xs[0], other)
    near = [index_of(ys[dy], z, xs[dx], core) for dy, dx in PLANE_STEPS]
    near_plane = [ys[dy] * NX + xs[dx] for dy, dx in PLANE_STEPS]
    from_plane = [back_y[dy] * NX + back_x[dx] for dy, dx in PLANE_STEPS]
    line = [index_of(ys[0], zs[d], xs[0], core) for d in LINE_STEPS]
    line_z = [zs[d] for d in LINE_STEPS]
    places = range(PLANE - 1)
    steps = range(NZ - 1)

    for peer in line + near + [twin]:
        greet(peer)
    load_r = pltpu.make_async_copy(relations, rel_v, loads.at[0])
    load_r.start()

    kept = []

    def relation_first(ids, dq, mark):
        kept.append([(ebt_a[...], dq_a[...], meta[2:3, :]), (ebt[...], dq, ids)])
        kept.append(mark + mark_a[...])
        relation_part(other, *kept, csend)

    grad_v[...] = gradients(1, blocks, ept, own, query, meta, metap, tot, rb, rbt, relation_first)
    pl.semaphore_wait(pltpu.get_barrier_semaphore(), len(line) + len(near) + 1)

    swap = send(csend, crecv, s_core.at[0], s_core.at[1], twin)
    swap.start()
    relation_part(core, *kept, acc)
    swap.wait()
    both = acc[...] + crecv[...]
    acc[...] = both
    xsend[...] = both.astype(jnp.bfloat16).reshape(PLANE, SHARE, 16, LANES)

    xcopies = [send(xsend.at[near_plane[i]], xslot.at[i], s_xs.at[i], s_xr.at[i], near[i]) for i in places]
    for c in xcopies:
        c.start()
    acc_s, fresh = adagrad(et[...], state[...], grad_v[...])
    state_out[...] = acc_s
    et_out[...] = fresh
    for c in xcopies:
        c.wait()
    part = acc[pl.ds(plane * SHARE, SHARE)]
    for i in places:
        part = part + xslot[i].astype(jnp.float32)
    zpart[...] = part.reshape(OWNERS, 8, LANES)

    def zcopy(i, piece):
        return send(zpart.at[piece], zslot.at[i], s_zs.at[i], s_zr.at[i], line[i])

    def gcopy(i, owner):
        return send(zres.at[owner], zres.at[owner], s_gs.at[i], s_gr.at[owner], line[i])

    for i in steps:
        @pl.when(line_z[i] < OWNERS)
        def _():
            zcopy(i, line_z[i]).start()

    @pl.when(z < OWNERS)
    def _():
        for i in steps:
            zcopy(i, 0).wait_recv()
        total = zpart[z]
        for i in steps:
            total = total + zslot[i]
        zres[z] = total
        for i in steps:
            gcopy(i, z).start()

    for i in steps:
        @pl.when(line_z[i] < OWNERS)
        def _():
            zcopy(i, line_z[i]).wait_send()

    for o in range(OWNERS):
        @pl.when(z != o)
        def _():
            gcopy(0, o).wait_recv()

    whole = zres[...].reshape(SHARE, 16, LANES)
    tail = whole[SHARE - 1]
    rest = tail[0:8] - tail[0:8].astype(jnp.bfloat16).astype(jnp.float32)
    tail = jnp.concatenate([tail[0:8], jnp.where(plane == PLANE - 1, rest, tail[8:16])], axis=0)
    fin[plane] = whole.astype(jnp.bfloat16)
    fin[plane, SHARE - 1] = tail.astype(jnp.bfloat16)

    def ncopy(i, piece):
        return send(fin.at[piece], fin.at[piece], s_as.at[i], s_ar.at[i], near[i])

    def tcopy(piece, slot):
        return send(fin.at[piece], sib.at[piece], s_bs.at[slot], s_br.at[slot], twin)

    for i in places:
        ncopy(i, plane).start()
    tcopy(plane, PLANE - 1).start()

    @pl.when(z < OWNERS)
    def _():
        for i in steps:
            gcopy(i, z).wait_send()

    load_r.wait()
    for i in reversed(places):
        ncopy(i, from_plane[i]).wait_recv()
        tcopy(from_plane[i], i).start()

    width = rel_v.shape[1]
    full = width // LANES
    tall = width // 16
    edge = full * LANES

    def finish(kind, ref):
        summed = ref[...].reshape(TILES, 16, LANES).astype(jnp.float32)
        for j in range(full):
            piece = summed[j * tall : (j + 1) * tall].reshape(width, LANES)
            span = slice(j * LANES, (j + 1) * LANES)
            rel_out[kind, :, span] = rel_v[kind, :, span] - REL_RATE * piece
        side = jnp.concatenate([summed[full * tall + j] for j in range(4)], axis=1)
        rel_out[kind, :, edge:] = rel_v[kind, :, edge:] - REL_RATE * side.T[:width, :]

    finish(core, fin)
    for i in reversed(places):
        tcopy(from_plane[i], i).wait()
    tcopy(plane, PLANE - 1).wait()
    for i in places:
        ncopy(i, plane).wait_send()
    finish(other, sib)

    def losses(ref):
        tile = ref[PLANE - 1, SHARE - 1].astype(jnp.float32)
        sums = tile[0:1] + tile[8:9]
        for rnd in range(ROUNDS):
            span = slice(rnd, rnd + 1)
            loss_out[:, span] = sums[:, span] / tot[span, 0:1]

    @pl.when(core == 0)
    def _():
        losses(fin)

    @pl.when(core == 1)
    def _():
        losses(sib)


def on_device(tables, state, relations, partner, counts, positive, relation_ids):
    rows, width = tables.shape
    blocks = lax.axis_size("blk")
    depth = blocks.bit_length() - 1
    me = lax.axis_index("blk")
    f32, bf16, i32 = jnp.float32, jnp.bfloat16, jnp.int32
    shape = jax.ShapeDtypeStruct
    DMA = pltpu.SemaphoreType.DMA
    block_f, block_b, flat_b = shape((width, rows), f32), shape((width, rows), bf16), shape((rows, width), bf16)
    ops_b, small_i, tile_f = shape(relations.shape, bf16), shape((8, rows), i32), shape((8, LANES), f32)
    accum_f, mark_f = shape((1, rows), f32), shape((16, LANES), f32)
    partial = functools.partial

    offset = jnp.bitwise_xor(partner[:, 0], me)
    level = jnp.zeros((ROUNDS,), i32)
    for bit in range(1, depth):
        level = level + (offset >> bit > 0).astype(i32)

    def first(bit, *args):
        return pl.pallas_call(
            partial(exchange_first, bit),
            out_shape=(block_b, ops_b, ops_b, small_i, block_b, small_i, tile_f, flat_b, block_b),
            in_specs=[ANY, ANY, VMEM, VMEM, VMEM],
            out_specs=(VMEM,) * 9,
            scratch_shapes=[
                pltpu.VMEM((width, rows), f32),
                pltpu.VMEM(relations.shape, f32),
                pltpu.VMEM((8, LANES), f32),
                pltpu.VMEM((8, LANES), f32),
                pltpu.VMEM((2 * PLANE - 1, 8, LANES), f32),
                pltpu.VMEM((NZ - 1, 8, LANES), f32),
                DMA((2,)),
                DMA((4,)),
                DMA((2 * PLANE - 1,)), DMA((2 * PLANE - 1,)),
                DMA((NZ - 1,)), DMA((NZ - 1,)),
            ],
            compiler_params=pltpu.CompilerParams(collective_id=bit, has_side_effects=True),
            name="swap_a",
        )(*args)

    def following(bit, *args):
        return pl.pallas_call(
            partial(exchange_next, bit),
            out_shape=(block_b, small_i, flat_b, block_b),
            in_specs=[VMEM] * 3,
            out_specs=(VMEM,) * 4,
            scratch_shapes=[DMA((4,))],
            compiler_params=pltpu.CompilerParams(collective_id=depth + bit, has_side_effects=True),
            name="swap_b",
        )(*args)

    et = tables.T
    accum = state.reshape(1, rows)
    ebt, rb, rbt, meta, ept, metap, tot, own, query = lax.switch(
        level[0], [partial(first, bit) for bit in range(depth)],
        et, relations, positive, relation_ids, counts.T)
    et, ebt2, accum, dq, mark = pl.pallas_call(
        partial(round_kernel, float(blocks)),
        out_shape=(block_f, block_b, accum_f, block_b, mark_f),
        in_specs=[ANY] + [VMEM] * 9,
        out_specs=(VMEM,) * 5,
        scratch_shapes=[pltpu.VMEM((width, rows), f32), DMA((1,))],
        name="round_a",
    )(et, ept, own, query, meta, metap, tot, accum, rb, rbt)

    ept, metap, own, query = lax.switch(
        level[1], [partial(following, bit) for bit in range(depth)],
        ebt2, meta, rbt)
    et, accum, relations_out, losses = pl.pallas_call(
        partial(last_kernel, float(blocks)),
        out_shape=(block_f, accum_f, shape(relations.shape, f32), shape((1, ROUNDS), f32)),
        in_specs=[VMEM] * 14 + [ANY],
        out_specs=(VMEM,) * 4,
        scratch_shapes=[
            pltpu.VMEM(relations.shape, f32),
            pltpu.VMEM((width, rows), f32),
            pltpu.VMEM((TILES, 16, LANES), f32),
            pltpu.VMEM((TILES, 16, LANES), f32),
            pltpu.VMEM((TILES, 16, LANES), f32),
            pltpu.VMEM((PLANE, SHARE, 16, LANES), bf16),
            pltpu.VMEM((PLANE - 1, SHARE, 16, LANES), bf16),
            pltpu.VMEM((OWNERS, 8, LANES), f32),
            pltpu.VMEM((NZ - 1, 8, LANES), f32),
            pltpu.VMEM((OWNERS, 8, LANES), f32),
            pltpu.VMEM((PLANE, SHARE, 16, LANES), bf16),
            pltpu.VMEM((PLANE, SHARE, 16, LANES), bf16),
            DMA((1,)),
            DMA((2,)),
            DMA((PLANE - 1,)), DMA((PLANE - 1,)),
            DMA((NZ - 1,)), DMA((NZ - 1,)),
            DMA((NZ - 1,)), DMA((OWNERS,)),
            DMA((PLANE - 1,)), DMA((PLANE - 1,)),
            DMA((PLANE,)), DMA((PLANE,)),
        ],
        compiler_params=pltpu.CompilerParams(collective_id=2 * depth, has_side_effects=True),
        name="last",
    )(et, ebt2, ept, own, query, meta, metap, tot, accum, rb, rbt, ebt, dq, mark, relations)
    return (et.T, accum.reshape(rows), relations_out, losses.reshape(ROUNDS))


def solution(mesh):
    return jax.shard_map(
        on_device,
        mesh=mesh,
        in_specs=(
            P("blk", None),
            P("blk"),
            P(),
            P(None, "blk"),
            P(None, "blk"),
            P(None, "blk"),
            P(None, "blk"),
        ),
        out_specs=(P("blk", None), P("blk"), P(), P()),
        check_vma=False,
    )
```

```python
import functools

import jax
import jax.numpy as jnp
from jax import lax
from jax.experimental import pallas as pl
from jax.experimental.pallas import tpu as pltpu
from jax.sharding import PartitionSpec as P

ROUNDS = 2
LEARN_RATE = 0.3
REL_RATE = 0.1
MESH = pl.DeviceIdType.MESH

NY, NZ, NX = 4, 16, 4
PLANE = NY * NX
LANES = 128
TILES = 80
SHARE = TILES // PLANE
OWNERS = SHARE * 2

VMEM = pl.BlockSpec(memory_space=pltpu.VMEM)
ANY = pl.BlockSpec(memory_space=pl.ANY)


def dot_nn(a, b):
    return lax.dot_general(a, b, (((1,), (0,)), ((), ())), preferred_element_type=jnp.float32)


def dot_nt(a, b):
    return lax.dot_general(a, b, (((1,), (1,)), ((), ())), preferred_element_type=jnp.float32)


def eye(n):
    rows = lax.broadcasted_iota(jnp.int32, (n, n), 0)
    return (rows == lax.broadcasted_iota(jnp.int32, (n, n), 1)).astype(jnp.bfloat16)


def coords():
    me = lax.axis_index("blk")
    core = lax.rem(me, 2)
    x = lax.rem(lax.div(me, 2), NX)
    z = lax.rem(lax.div(me, 2 * NX), NZ)
    y = lax.div(me, 2 * NX * NZ)
    return y, z, x, core


def spots():
    y, z, x, core = coords()
    ys = [lax.rem(y + d, NY) for d in range(NY)]
    zs = [lax.rem(z + d, NZ) for d in range(NZ)]
    xs = [lax.rem(x + d, NX) for d in range(NX)]
    return ys, zs, xs, core


def index_of(y, z, x, core):
    return y * (2 * NX * NZ) + z * (2 * NX) + x * 2 + core


def hops(d, size):
    return min(d, size - d)


PLANE_STEPS = sorted(
    [(dy, dx) for dy in range(NY) for dx in range(NX) if dy or dx],
    key=lambda s: -(hops(s[0], NY) + hops(s[1], NX)))
LINE_STEPS = sorted(range(1, NZ), key=lambda d: -hops(d, NZ))
REACH = 4
SHORT_STEPS = [d for d in LINE_STEPS if hops(d, NZ) <= REACH]


def greet(peer):
    pl.semaphore_signal(
        pltpu.get_barrier_semaphore(), inc=1, device_id=(peer,), device_id_type=MESH)


def send(src, dst, send_sem, recv_sem, peer):
    return pltpu.make_async_remote_copy(
        src, dst, send_sem, recv_sem, device_id=(peer,), device_id_type=MESH)


def pair_of(bit):
    me = lax.axis_index("blk")
    step = 1 << bit
    return me + step * (1 - 2 * lax.rem(lax.div(me, step), 2))


def own_forms(ebt, rbt, ids, own, query):
    own_t = ebt[...]
    own[...] = dot_nt(eye(own_t.shape[1]), own_t).astype(jnp.bfloat16)
    parts = [dot_nn(rbt[k], own_t) for k in range(rbt.shape[0])]
    query[...] = pick(ids, parts).astype(jnp.bfloat16)


def exchange_first(bit, et, relations, positive, relation_ids, counts,
                   ebt, rb, rbt, meta, ept, metap, tot, own, query,
                   et_v, rel_v, cnt, part, aslot, bslot, ends, cslot,
                   loads, sems, asend, arecv, bsend, brecv, csend, crecv):
    ys, zs, xs, core = spots()
    partner = pair_of(bit)
    load_e = pltpu.make_async_copy(et, et_v, loads.at[0])
    load_r = pltpu.make_async_copy(relations, rel_v, loads.at[1])
    load_e.start()
    load_r.start()

    near = [index_of(ys[dy], zs[0], xs[dx], core) for dy, dx in PLANE_STEPS]
    near += [index_of(ys[dy], zs[0], xs[dx], 1 - core) for dy, dx in PLANE_STEPS]
    near += [index_of(ys[0], zs[0], xs[0], 1 - core)]
    line = [index_of(ys[0], zs[d], xs[0], core) for d in SHORT_STEPS]
    for peer in line + near + [partner]:
        greet(peer)

    meta[0:2, :] = positive[...]
    meta[2:4, :] = relation_ids[...]
    cnt[...] = jnp.zeros(cnt.shape, jnp.float32)
    for rnd in range(ROUNDS):
        one = counts[0:1, rnd : rnd + 1]
        meta[4 + rnd : 5 + rnd, :] = jnp.broadcast_to(one, (1, meta.shape[1]))
        meta[6 + rnd : 7 + rnd, :] = jnp.broadcast_to(one, (1, meta.shape[1]))
        cnt[rnd : rnd + 1, :] = jnp.broadcast_to(one.astype(jnp.float32), (1, LANES))
    load_e.wait()
    ebt[...] = et_v[...].astype(jnp.bfloat16)
    pl.semaphore_wait(pltpu.get_barrier_semaphore(), len(line) + len(near) + 1)

    acopies = [send(cnt, aslot.at[i], asend.at[i], arecv.at[i], peer) for i, peer in enumerate(near)]
    bcopies = [send(part, bslot.at[i], bsend.at[i], brecv.at[i], peer) for i, peer in enumerate(line)]
    small = send(meta, metap, sems.at[2], sems.at[3], partner)
    block = send(ebt, ept, sems.at[0], sems.at[1], partner)
    for c in acopies:
        c.start()
    small.start()
    block.start()

    load_r.wait()
    ident = eye(rb.shape[1])
    for kind in range(rb.shape[0]):
        op = rel_v[kind].astype(jnp.bfloat16)
        rb[kind] = op
        rbt[kind] = dot_nt(ident, op).astype(jnp.bfloat16)

    for c in acopies:
        c.wait()
    part[...] = cnt[...] + jnp.sum(aslot[...], axis=0)
    for c in bcopies:
        c.start()
    own_forms(ebt, rbt, meta[2:3, :], own, query)
    for c in bcopies:
        c.wait()
    ahead = sum(bslot[i] for i, d in enumerate(SHORT_STEPS) if d >= NZ - REACH)
    behind = sum(bslot[i] for i, d in enumerate(SHORT_STEPS) if d < REACH)
    ends[0] = ahead
    ends[1] = behind
    backward, forward = line[SHORT_STEPS.index(NZ - REACH)], line[SHORT_STEPS.index(REACH)]
    ccopies = [send(ends.at[i], cslot.at[i], csend.at[i], crecv.at[i], peer)
               for i, peer in enumerate((backward, forward))]
    for c in ccopies:
        c.start()
    near_sum = part[...] + jnp.sum(bslot[...], axis=0)
    for c in ccopies:
        c.wait()
    tot[...] = near_sum + cslot[0] + cslot[1]
    small.wait()
    block.wait()


def exchange_next(bit, ebt, meta, rbt, ept, metap, own, query, sems):
    partner = pair_of(bit)
    greet(partner)
    pl.semaphore_wait(pltpu.get_barrier_semaphore(), 1)
    small = send(meta, metap, sems.at[2], sems.at[3], partner)
    block = send(ebt, ept, sems.at[0], sems.at[1], partner)
    small.start()
    block.start()
    own_forms(ebt, rbt, meta[3:4, :], own, query)
    small.wait()
    block.wait()


def pick(ids, parts):
    out = parts[0]
    for kind in range(1, len(parts)):
        out = jnp.where(ids == kind, parts[kind], out)
    return out


def bucket(dst, query_t, pos, count, weight):
    scores = dot_nn(dst, query_t)
    top = jnp.max(scores, axis=0, keepdims=True)
    shifted = jnp.exp(scores - top)
    denom = jnp.sum(shifted, axis=0, keepdims=True)
    hit = lax.broadcasted_iota(jnp.int32, scores.shape, 0) == pos
    aim = jnp.sum(jnp.where(hit, scores, 0.0), axis=0, keepdims=True)
    valid = lax.broadcasted_iota(jnp.int32, pos.shape, 1) < count
    scale = jnp.where(valid, weight, 0.0)
    slope = scale * (shifted * (1.0 / denom) - jnp.where(hit, 1.0, 0.0))
    rows = jnp.where(valid, jnp.log(denom) + top - aim, 0.0)
    return slope.astype(jnp.bfloat16), rows


def relation_part(kind, rounds, mark, out):
    width = rounds[0][0].shape[0]
    full, tall = width // LANES, width // 16
    main = side = 0.0
    for own_t, dq, ids in rounds:
        picked = jnp.where(ids == kind, own_t, jnp.zeros_like(own_t))
        main = main + dot_nt(picked, dq)
        side = side + dot_nt(dq[full * LANES :, :], picked)
    side = jnp.concatenate([side, jnp.zeros((16, 4 * LANES - width), jnp.float32)], axis=1)
    for j in range(full):
        out[j * tall : (j + 1) * tall] = main[:, j * LANES : (j + 1) * LANES].reshape(tall, 16, LANES)
    for j in range(4):
        out[full * tall + j] = side[:, j * LANES : (j + 1) * LANES]
    out[TILES - 1] = jnp.where(kind == 0, mark, 0.0)


def loss_mark(loss, rnd):
    total = jnp.sum(loss, axis=1, keepdims=True)
    lane = lax.broadcasted_iota(jnp.int32, (16, LANES), 1)
    row = lax.broadcasted_iota(jnp.int32, (16, LANES), 0)
    return jnp.where((lane == rnd) & (row == 0), jnp.broadcast_to(total, (16, LANES)), 0.0)


def gradients(rnd, blocks, ept, own, query, meta, metap, tot, rb, rbt, then):
    kinds = rb.shape[0]
    far_t = ept[...]
    far = dot_nt(eye(far_t.shape[1]), far_t).astype(jnp.bfloat16)
    weight = blocks / tot[rnd : rnd + 1, 0:1]
    pos, ids, count = meta[rnd : rnd + 1, :], meta[2 + rnd : 3 + rnd, :], meta[4 + rnd : 5 + rnd, :]
    pos_p, ids_p = metap[rnd : rnd + 1, :], metap[2 + rnd : 3 + rnd, :]
    count_p = metap[4 + rnd : 5 + rnd, :]

    slope, loss = bucket(far, query[...], pos, count, weight)
    dq = dot_nn(far_t, slope).astype(jnp.bfloat16)
    then(ids, dq, loss_mark(loss, rnd))
    query_p = pick(ids_p, [dot_nn(rbt[k], far_t) for k in range(kinds)]).astype(jnp.bfloat16)
    slope_p, _ = bucket(own[...], query_p, pos_p, count_p, weight)
    grad = pick(ids, [dot_nn(rb[k], dq) for k in range(kinds)])
    return grad + dot_nt(query_p, slope_p).astype(jnp.bfloat16).astype(jnp.float32)


def adagrad(et, state, grad):
    acc = state + jnp.mean(grad * grad, axis=0, keepdims=True)
    return acc, et - LEARN_RATE * grad / jnp.sqrt(acc)


def round_kernel(blocks, et, ept, own, query, meta, metap, tot, state, rb, rbt,
                 et_out, ebt_out, state_out, dq_out, mark_out, et_v, loads):
    load_e = pltpu.make_async_copy(et, et_v, loads.at[0])
    load_e.start()

    def keep(ids, dq, mark):
        dq_out[...] = dq
        mark_out[...] = mark

    grad = gradients(0, blocks, ept, own, query, meta, metap, tot, rb, rbt, keep)
    load_e.wait()
    acc, fresh = adagrad(et_v[...], state[...], grad)
    state_out[...] = acc
    et_out[...] = fresh
    ebt_out[...] = fresh.astype(jnp.bfloat16)


def last_kernel(blocks, et, ebt, ept, own, query, meta, metap, tot, state, rb, rbt, ebt_a, dq_a, mark_a,
                et_out, state_out, summed,
                grad_v, csend, crecv, acc, xsend, xslot, zpart, zslot, zres,
                s_core, s_xs, s_xr, s_zs, s_zr, s_gs, s_gr, s_as, s_ar, s_bs, s_br):
    ys, zs, xs, core = spots()
    back_y = [lax.rem(ys[0] + NY - d, NY) for d in range(NY)]
    back_x = [lax.rem(xs[0] + NX - d, NX) for d in range(NX)]
    z = zs[0]
    plane = ys[0] * NX + xs[0]
    other = 1 - core
    twin = index_of(ys[0], z, xs[0], other)
    near = [index_of(ys[dy], z, xs[dx], core) for dy, dx in PLANE_STEPS]
    near_plane = [ys[dy] * NX + xs[dx] for dy, dx in PLANE_STEPS]
    from_plane = [back_y[dy] * NX + back_x[dx] for dy, dx in PLANE_STEPS]
    line = [index_of(ys[0], zs[d], xs[0], core) for d in LINE_STEPS]
    line_z = [zs[d] for d in LINE_STEPS]
    places = range(PLANE - 1)
    steps = range(NZ - 1)

    for peer in line + near + [twin]:
        greet(peer)
    kept = []

    def relation_first(ids, dq, mark):
        kept.append([(ebt_a[...], dq_a[...], meta[2:3, :]), (ebt[...], dq, ids)])
        kept.append(mark + mark_a[...])
        relation_part(other, *kept, csend)

    grad_v[...] = gradients(1, blocks, ept, own, query, meta, metap, tot, rb, rbt, relation_first)
    pl.semaphore_wait(pltpu.get_barrier_semaphore(), len(line) + len(near) + 1)

    swap = send(csend, crecv, s_core.at[0], s_core.at[1], twin)
    swap.start()
    relation_part(core, *kept, acc)
    swap.wait()
    both = acc[...] + crecv[...]
    acc[...] = both
    xsend[...] = both.astype(jnp.bfloat16).reshape(PLANE, SHARE, 16, LANES)

    xcopies = [send(xsend.at[near_plane[i]], xslot.at[i], s_xs.at[i], s_xr.at[i], near[i]) for i in places]
    for c in xcopies:
        c.start()
    acc_s, fresh = adagrad(et[...], state[...], grad_v[...])
    state_out[...] = acc_s
    et_out[...] = fresh
    for c in xcopies:
        c.wait()
    part = acc[pl.ds(plane * SHARE, SHARE)]
    for i in places:
        part = part + xslot[i].astype(jnp.float32)
    zpart[...] = part.reshape(OWNERS, 8, LANES)

    def zcopy(i, piece):
        return send(zpart.at[piece], zslot.at[i], s_zs.at[i], s_zr.at[i], line[i])

    def gcopy(i, owner):
        return send(zres.at[owner], zres.at[owner], s_gs.at[i], s_gr.at[owner], line[i])

    for i in steps:
        @pl.when(line_z[i] < OWNERS)
        def _():
            zcopy(i, line_z[i]).start()

    @pl.when(z < OWNERS)
    def _():
        for i in steps:
            zcopy(i, 0).wait_recv()
        total = zpart[z]
        for i in steps:
            total = total + zslot[i]
        zres[z] = total
        for i in steps:
            gcopy(i, z).start()

    for i in steps:
        @pl.when(line_z[i] < OWNERS)
        def _():
            zcopy(i, line_z[i]).wait_send()

    for o in range(OWNERS):
        @pl.when(z != o)
        def _():
            gcopy(0, o).wait_recv()

    whole = zres[...].reshape(SHARE, 16, LANES)
    tail = whole[SHARE - 1]
    rest = tail[0:8] - tail[0:8].astype(jnp.bfloat16).astype(jnp.float32)
    tail = jnp.concatenate([tail[0:8], jnp.where(plane == PLANE - 1, rest, tail[8:16])], axis=0)
    summed[core, plane] = whole.astype(jnp.bfloat16)
    summed[core, plane, SHARE - 1] = tail.astype(jnp.bfloat16)

    def ncopy(i, piece):
        return send(summed.at[core, piece], summed.at[core, piece], s_as.at[i], s_ar.at[i], near[i])

    def tcopy(piece, slot):
        return send(summed.at[core, piece], summed.at[core, piece], s_bs.at[slot], s_br.at[slot], twin)

    for i in places:
        ncopy(i, plane).start()
    tcopy(plane, PLANE - 1).start()

    @pl.when(z < OWNERS)
    def _():
        for i in steps:
            gcopy(i, z).wait_send()

    for i in reversed(places):
        ncopy(i, from_plane[i]).wait_recv()
        tcopy(from_plane[i], i).start()
    for i in places:
        ncopy(i, plane).wait_send()

    def arrived(piece, slot):
        return send(summed.at[other, piece], summed.at[other, piece], s_bs.at[slot], s_br.at[slot], twin)

    for i in reversed(places):
        tcopy(from_plane[i], i).wait_send()
        arrived(from_plane[i], i).wait_recv()
    tcopy(plane, PLANE - 1).wait_send()
    arrived(plane, PLANE - 1).wait_recv()


def finish_kernel(et, summed, relations, tot, state, et_out, rel_out, loss_out, state_out, rel_v, out_v, sems):
    kinds, width = relations.shape[:2]
    full, tall = width // LANES, width // 16
    edge = full * LANES
    table = pltpu.make_async_copy(et, et_out, sems.at[0])
    table.start()
    loads = [pltpu.make_async_copy(relations.at[k], rel_v.at[k], sems.at[1 + k]) for k in range(kinds)]
    stores = [pltpu.make_async_copy(out_v.at[k], rel_out.at[k], sems.at[1 + kinds + k]) for k in range(kinds)]
    for c in loads:
        c.start()
    state_out[...] = state[...]
    tile = summed[0, PLANE - 1, SHARE - 1].astype(jnp.float32)
    sums = tile[0:1] + tile[8:9]
    for rnd in range(ROUNDS):
        span = slice(rnd, rnd + 1)
        loss_out[:, span] = sums[:, span] / tot[span, 0:1]
    for kind in range(kinds):
        loads[kind].wait()
        total = summed[kind].reshape(TILES, 16, LANES).astype(jnp.float32)
        for j in range(full):
            piece = total[j * tall : (j + 1) * tall].reshape(width, LANES)
            span = slice(j * LANES, (j + 1) * LANES)
            out_v[kind, :, span] = rel_v[kind, :, span] - REL_RATE * piece
        side = jnp.concatenate([total[full * tall + j] for j in range(4)], axis=1)
        out_v[kind, :, edge:] = rel_v[kind, :, edge:] - REL_RATE * side.T[:width, :]
        stores[kind].start()
    for c in stores:
        c.wait()
    table.wait()


def on_device(tables, state, relations, partner, counts, positive, relation_ids):
    rows, width = tables.shape
    blocks = lax.axis_size("blk")
    depth = blocks.bit_length() - 1
    me = lax.axis_index("blk")
    f32, bf16, i32 = jnp.float32, jnp.bfloat16, jnp.int32
    shape = jax.ShapeDtypeStruct
    DMA = pltpu.SemaphoreType.DMA
    block_f, block_b, flat_b = shape((width, rows), f32), shape((width, rows), bf16), shape((rows, width), bf16)
    ops_b, small_i, tile_f = shape(relations.shape, bf16), shape((8, rows), i32), shape((8, LANES), f32)
    accum_f, mark_f = shape((1, rows), f32), shape((16, LANES), f32)
    partial = functools.partial

    def level(rnd):
        offset = jnp.bitwise_xor(partner[rnd, 0], me)
        return sum((offset >> bit > 0).astype(i32) for bit in range(1, depth))

    def first(bit, *args):
        return pl.pallas_call(
            partial(exchange_first, bit),
            out_shape=(block_b, ops_b, ops_b, small_i, block_b, small_i, tile_f, flat_b, block_b),
            in_specs=[ANY, ANY, VMEM, VMEM, VMEM],
            out_specs=(VMEM,) * 9,
            scratch_shapes=[
                pltpu.VMEM((width, rows), f32),
                pltpu.VMEM(relations.shape, f32),
                pltpu.VMEM((8, LANES), f32),
                pltpu.VMEM((8, LANES), f32),
                pltpu.VMEM((2 * PLANE - 1, 8, LANES), f32),
                pltpu.VMEM((2 * REACH, 8, LANES), f32),
                pltpu.VMEM((2, 8, LANES), f32),
                pltpu.VMEM((2, 8, LANES), f32),
                DMA((2,)),
                DMA((4,)),
                DMA((2 * PLANE - 1,)), DMA((2 * PLANE - 1,)),
                DMA((2 * REACH,)), DMA((2 * REACH,)),
                DMA((2,)), DMA((2,)),
            ],
            compiler_params=pltpu.CompilerParams(collective_id=bit, has_side_effects=True),
            name="swap_a",
        )(*args)

    def following(bit, *args):
        return pl.pallas_call(
            partial(exchange_next, bit),
            out_shape=(block_b, small_i, flat_b, block_b),
            in_specs=[VMEM] * 3,
            out_specs=(VMEM,) * 4,
            scratch_shapes=[DMA((4,))],
            compiler_params=pltpu.CompilerParams(collective_id=depth + bit, has_side_effects=True),
            name="swap_b",
        )(*args)

    et = tables.T
    accum = state.reshape(1, rows)
    ebt, rb, rbt, meta, ept, metap, tot, own, query = lax.switch(
        level(0), [partial(first, bit) for bit in range(depth)],
        et, relations, positive, relation_ids, counts.T)
    et, ebt2, accum, dq, mark = pl.pallas_call(
        partial(round_kernel, float(blocks)),
        out_shape=(block_f, block_b, accum_f, block_b, mark_f),
        in_specs=[ANY] + [VMEM] * 9,
        out_specs=(VMEM,) * 5,
        scratch_shapes=[pltpu.VMEM((width, rows), f32), DMA((1,))],
        name="round_a",
    )(et, ept, own, query, meta, metap, tot, accum, rb, rbt)

    ept, metap, own, query = lax.switch(
        level(1), [partial(following, bit) for bit in range(depth)],
        ebt2, meta, rbt)
    et, accum_v, summed = pl.pallas_call(
        partial(last_kernel, float(blocks)),
        out_shape=(block_f, accum_f, shape((2, PLANE, SHARE, 16, LANES), bf16)),
        in_specs=[VMEM] * 14,
        out_specs=(VMEM,) * 3,
        scratch_shapes=[
            pltpu.VMEM((width, rows), f32),
            pltpu.VMEM((TILES, 16, LANES), f32),
            pltpu.VMEM((TILES, 16, LANES), f32),
            pltpu.VMEM((TILES, 16, LANES), f32),
            pltpu.VMEM((PLANE, SHARE, 16, LANES), bf16),
            pltpu.VMEM((PLANE - 1, SHARE, 16, LANES), bf16),
            pltpu.VMEM((OWNERS, 8, LANES), f32),
            pltpu.VMEM((NZ - 1, 8, LANES), f32),
            pltpu.VMEM((OWNERS, 8, LANES), f32),
            DMA((2,)),
            DMA((PLANE - 1,)), DMA((PLANE - 1,)),
            DMA((NZ - 1,)), DMA((NZ - 1,)),
            DMA((NZ - 1,)), DMA((OWNERS,)),
            DMA((PLANE - 1,)), DMA((PLANE - 1,)),
            DMA((PLANE,)), DMA((PLANE,)),
        ],
        compiler_params=pltpu.CompilerParams(collective_id=2 * depth, has_side_effects=True),
        name="last",
    )(et, ebt2, ept, own, query, meta, metap, tot, accum, rb, rbt, ebt, dq, mark)
    et, relations_out, losses, accum = pl.pallas_call(
        finish_kernel,
        out_shape=(block_f, shape(relations.shape, f32), shape((1, ROUNDS), f32), accum_f),
        in_specs=[VMEM, VMEM, ANY, VMEM, VMEM],
        out_specs=(ANY, ANY, VMEM, VMEM),
        scratch_shapes=[
            pltpu.VMEM(relations.shape, f32), pltpu.VMEM(relations.shape, f32), DMA((5,)),
        ],
        name="finish",
    )(et, summed, relations, tot, accum_v)
    return (et.T, accum.reshape(rows), relations_out, losses.reshape(ROUNDS))


def solution(mesh):
    return jax.shard_map(
        on_device,
        mesh=mesh,
        in_specs=(
            P("blk", None),
            P("blk"),
            P(),
            P(None, "blk"),
            P(None, "blk"),
            P(None, "blk"),
            P(None, "blk"),
        ),
        out_specs=(P("blk", None), P("blk"), P(), P()),
        check_vma=False,
    )
```

```python
import functools

import jax
import jax.numpy as jnp
from jax import lax
from jax.experimental import pallas as pl
from jax.experimental.pallas import tpu as pltpu
from jax.sharding import PartitionSpec as P

ROUNDS = 2
LEARN_RATE = 0.3
REL_RATE = 0.1
MESH = pl.DeviceIdType.MESH

NY, NZ, NX = 4, 16, 4
PLANE = NY * NX
LANES = 128
TILES = 80
SHARE = TILES // PLANE
OWNERS = SHARE * 2

GRANT = 20 * 2**20

VMEM = pl.BlockSpec(memory_space=pltpu.VMEM)
ANY = pl.BlockSpec(memory_space=pl.ANY)


def dot_nn(a, b):
    return lax.dot_general(a, b, (((1,), (0,)), ((), ())), preferred_element_type=jnp.float32)


def dot_nt(a, b):
    return lax.dot_general(a, b, (((1,), (1,)), ((), ())), preferred_element_type=jnp.float32)


def eye(n):
    rows = lax.broadcasted_iota(jnp.int32, (n, n), 0)
    return (rows == lax.broadcasted_iota(jnp.int32, (n, n), 1)).astype(jnp.bfloat16)


def coords():
    me = lax.axis_index("blk")
    core = lax.rem(me, 2)
    x = lax.rem(lax.div(me, 2), NX)
    z = lax.rem(lax.div(me, 2 * NX), NZ)
    y = lax.div(me, 2 * NX * NZ)
    return y, z, x, core


def spots():
    y, z, x, core = coords()
    ys = [lax.rem(y + d, NY) for d in range(NY)]
    zs = [lax.rem(z + d, NZ) for d in range(NZ)]
    xs = [lax.rem(x + d, NX) for d in range(NX)]
    return ys, zs, xs, core


def index_of(y, z, x, core):
    return y * (2 * NX * NZ) + z * (2 * NX) + x * 2 + core


def hops(d, size):
    return min(d, size - d)


PLANE_STEPS = sorted(
    [(dy, dx) for dy in range(NY) for dx in range(NX) if dy or dx],
    key=lambda s: -(hops(s[0], NY) + hops(s[1], NX)))
LINE_STEPS = sorted(range(1, NZ), key=lambda d: -hops(d, NZ))
REACH = 4
SHORT_STEPS = [d for d in LINE_STEPS if hops(d, NZ) <= REACH]


def greet(peer):
    pl.semaphore_signal(
        pltpu.get_barrier_semaphore(), inc=1, device_id=(peer,), device_id_type=MESH)


def send(src, dst, send_sem, recv_sem, peer):
    return pltpu.make_async_remote_copy(
        src, dst, send_sem, recv_sem, device_id=(peer,), device_id_type=MESH)


def pair_of(bit):
    me = lax.axis_index("blk")
    step = 1 << bit
    return me + step * (1 - 2 * lax.rem(lax.div(me, step), 2))


def own_forms(ebt, rbt, ids, own, query, own_v, query_v, stores):
    own_t = ebt[...]
    own_v[...] = dot_nt(eye(own_t.shape[1]), own_t).astype(jnp.bfloat16)
    out = pltpu.make_async_copy(own_v, own, stores.at[0])
    out.start()
    parts = [dot_nn(rbt[k], own_t) for k in range(rbt.shape[0])]
    query_v[...] = pick(ids, parts).astype(jnp.bfloat16)
    out_q = pltpu.make_async_copy(query_v, query, stores.at[1])
    out_q.start()
    return out, out_q


def exchange_first(bit, et, relations, positive, relation_ids, counts,
                   ebt, rb, rbt, meta, ept, metap, tot, own, query,
                   ebt_v, own_v, query_v, stores, et_v, rel_v, cnt, part, aslot, bslot, ends, cslot,
                   loads, sems, asend, arecv, bsend, brecv, csend, crecv):
    ys, zs, xs, core = spots()
    partner = pair_of(bit)
    load_e = pltpu.make_async_copy(et, et_v, loads.at[0])
    load_r = pltpu.make_async_copy(relations, rel_v, loads.at[1])
    load_e.start()
    load_r.start()

    near = [index_of(ys[dy], zs[0], xs[dx], core) for dy, dx in PLANE_STEPS]
    near += [index_of(ys[dy], zs[0], xs[dx], 1 - core) for dy, dx in PLANE_STEPS]
    near += [index_of(ys[0], zs[0], xs[0], 1 - core)]
    line = [index_of(ys[0], zs[d], xs[0], core) for d in SHORT_STEPS]
    for peer in line + near + [partner]:
        greet(peer)

    meta[0:2, :] = positive[...]
    meta[2:4, :] = relation_ids[...]
    cnt[...] = jnp.zeros(cnt.shape, jnp.float32)
    for rnd in range(ROUNDS):
        one = counts[0:1, rnd : rnd + 1]
        meta[4 + rnd : 5 + rnd, :] = jnp.broadcast_to(one, (1, meta.shape[1]))
        meta[6 + rnd : 7 + rnd, :] = jnp.broadcast_to(one, (1, meta.shape[1]))
        cnt[rnd : rnd + 1, :] = jnp.broadcast_to(one.astype(jnp.float32), (1, LANES))
    load_e.wait()
    ebt_v[...] = et_v[...].astype(jnp.bfloat16)
    pl.semaphore_wait(pltpu.get_barrier_semaphore(), len(line) + len(near) + 1)

    acopies = [send(cnt, aslot.at[i], asend.at[i], arecv.at[i], peer) for i, peer in enumerate(near)]
    bcopies = [send(part, bslot.at[i], bsend.at[i], brecv.at[i], peer) for i, peer in enumerate(line)]
    small = send(meta, metap, sems.at[2], sems.at[3], partner)
    block = send(ebt_v, ept, sems.at[0], sems.at[1], partner)
    for c in acopies:
        c.start()
    small.start()
    block.start()
    keep = pltpu.make_async_copy(ebt_v, ebt, stores.at[2])
    keep.start()

    load_r.wait()
    ident = eye(rb.shape[1])
    for kind in range(rb.shape[0]):
        op = rel_v[kind].astype(jnp.bfloat16)
        rb[kind] = op
        rbt[kind] = dot_nt(ident, op).astype(jnp.bfloat16)

    for c in acopies:
        c.wait()
    part[...] = cnt[...] + jnp.sum(aslot[...], axis=0)
    for c in bcopies:
        c.start()
    outs = own_forms(ebt_v, rbt, meta[2:3, :], own, query, own_v, query_v, stores)
    for c in bcopies:
        c.wait()
    ahead = sum(bslot[i] for i, d in enumerate(SHORT_STEPS) if d >= NZ - REACH)
    behind = sum(bslot[i] for i, d in enumerate(SHORT_STEPS) if d < REACH)
    ends[0] = ahead
    ends[1] = behind
    backward, forward = line[SHORT_STEPS.index(NZ - REACH)], line[SHORT_STEPS.index(REACH)]
    ccopies = [send(ends.at[i], cslot.at[i], csend.at[i], crecv.at[i], peer)
               for i, peer in enumerate((backward, forward))]
    for c in ccopies:
        c.start()
    near_sum = part[...] + jnp.sum(bslot[...], axis=0)
    for c in ccopies:
        c.wait()
    tot[...] = near_sum + cslot[0] + cslot[1]
    for c in (keep, *outs):
        c.wait()
    small.wait()
    block.wait()


def exchange_next(bit, ebt, meta, rbt, ept, metap, own, query, own_v, query_v, stores, sems):
    partner = pair_of(bit)
    greet(partner)
    pl.semaphore_wait(pltpu.get_barrier_semaphore(), 1)
    small = send(meta, metap, sems.at[2], sems.at[3], partner)
    block = send(ebt, ept, sems.at[0], sems.at[1], partner)
    small.start()
    block.start()
    outs = own_forms(ebt, rbt, meta[3:4, :], own, query, own_v, query_v, stores)
    for c in outs:
        c.wait()
    small.wait()
    block.wait()


def pick(ids, parts):
    out = parts[0]
    for kind in range(1, len(parts)):
        out = jnp.where(ids == kind, parts[kind], out)
    return out


def bucket(dst, query_t, pos, count, weight):
    scores = dot_nn(dst, query_t)
    top = jnp.max(scores, axis=0, keepdims=True)
    shifted = jnp.exp(scores - top)
    denom = jnp.sum(shifted, axis=0, keepdims=True)
    hit = lax.broadcasted_iota(jnp.int32, scores.shape, 0) == pos
    aim = jnp.sum(jnp.where(hit, scores, 0.0), axis=0, keepdims=True)
    valid = lax.broadcasted_iota(jnp.int32, pos.shape, 1) < count
    scale = jnp.where(valid, weight, 0.0)
    slope = scale * (shifted * (1.0 / denom) - jnp.where(hit, 1.0, 0.0))
    rows = jnp.where(valid, jnp.log(denom) + top - aim, 0.0)
    return slope.astype(jnp.bfloat16), rows


def relation_part(kind, rounds, mark, out):
    width = rounds[0][0].shape[0]
    full, tall = width // LANES, width // 16
    main = side = 0.0
    for own_t, dq, ids in rounds:
        picked = jnp.where(ids == kind, own_t, jnp.zeros_like(own_t))
        main = main + dot_nt(picked, dq)
        side = side + dot_nt(dq[full * LANES :, :], picked)
    side = jnp.concatenate([side, jnp.zeros((16, 4 * LANES - width), jnp.float32)], axis=1)
    for j in range(full):
        out[j * tall : (j + 1) * tall] = main[:, j * LANES : (j + 1) * LANES].reshape(tall, 16, LANES)
    for j in range(4):
        out[full * tall + j] = side[:, j * LANES : (j + 1) * LANES]
    out[TILES - 1] = jnp.where(kind == 0, mark, 0.0)


def loss_mark(loss, rnd):
    total = jnp.sum(loss, axis=1, keepdims=True)
    lane = lax.broadcasted_iota(jnp.int32, (16, LANES), 1)
    row = lax.broadcasted_iota(jnp.int32, (16, LANES), 0)
    return jnp.where((lane == rnd) & (row == 0), jnp.broadcast_to(total, (16, LANES)), 0.0)


def gradients(rnd, blocks, ept, own, query, meta, metap, tot, rb, rbt, then):
    kinds = rb.shape[0]
    far_t = ept[...]
    far = dot_nt(eye(far_t.shape[1]), far_t).astype(jnp.bfloat16)
    weight = blocks / tot[rnd : rnd + 1, 0:1]
    pos, ids, count = meta[rnd : rnd + 1, :], meta[2 + rnd : 3 + rnd, :], meta[4 + rnd : 5 + rnd, :]
    pos_p, ids_p = metap[rnd : rnd + 1, :], metap[2 + rnd : 3 + rnd, :]
    count_p = metap[4 + rnd : 5 + rnd, :]

    slope, loss = bucket(far, query[...], pos, count, weight)
    dq = dot_nn(far_t, slope).astype(jnp.bfloat16)
    then(ids, dq, loss_mark(loss, rnd))
    query_p = pick(ids_p, [dot_nn(rbt[k], far_t) for k in range(kinds)]).astype(jnp.bfloat16)
    slope_p, _ = bucket(own[...], query_p, pos_p, count_p, weight)
    grad = pick(ids, [dot_nn(rb[k], dq) for k in range(kinds)])
    return grad + dot_nt(query_p, slope_p).astype(jnp.bfloat16).astype(jnp.float32)


def adagrad(et, state, grad):
    acc = state + jnp.mean(grad * grad, axis=0, keepdims=True)
    return acc, et - LEARN_RATE * grad / jnp.sqrt(acc)


def fetch(pairs, sems):
    copies = [pltpu.make_async_copy(src, dst, sems.at[i]) for i, (src, dst) in enumerate(pairs)]
    for c in copies:
        c.start()
    return copies


def round_kernel(blocks, et, ept_h, own_h, query_h, meta, metap, tot, state, rb, rbt,
                 et_out, ebt_out, state_out, dq_out, mark_out, ept, own, query, et_v, loads):
    *early, load_e = fetch([(ept_h, ept), (query_h, query), (own_h, own), (et, et_v)], loads)
    for c in early:
        c.wait()

    def keep(ids, dq, mark):
        dq_out[...] = dq
        mark_out[...] = mark

    grad = gradients(0, blocks, ept, own, query, meta, metap, tot, rb, rbt, keep)
    load_e.wait()
    acc, fresh = adagrad(et_v[...], state[...], grad)
    state_out[...] = acc
    et_out[...] = fresh
    ebt_out[...] = fresh.astype(jnp.bfloat16)


def last_kernel(blocks, et, ebt, ept_h, own_h, query_h, meta, metap, tot, state, rb, rbt, ebt_h, dq_a, mark_a,
                et_out, state_out, summed,
                ept, own, query, ebt_a, loads, grad_v, csend, crecv, acc, xsend, xslot, zpart, zslot, zres,
                s_core, s_xs, s_xr, s_zs, s_zr, s_gs, s_gr, s_as, s_ar, s_bs, s_br):
    ys, zs, xs, core = spots()
    back_y = [lax.rem(ys[0] + NY - d, NY) for d in range(NY)]
    back_x = [lax.rem(xs[0] + NX - d, NX) for d in range(NX)]
    z = zs[0]
    plane = ys[0] * NX + xs[0]
    other = 1 - core
    twin = index_of(ys[0], z, xs[0], other)
    near = [index_of(ys[dy], z, xs[dx], core) for dy, dx in PLANE_STEPS]
    near_plane = [ys[dy] * NX + xs[dx] for dy, dx in PLANE_STEPS]
    from_plane = [back_y[dy] * NX + back_x[dx] for dy, dx in PLANE_STEPS]
    line = [index_of(ys[0], zs[d], xs[0], core) for d in LINE_STEPS]
    line_z = [zs[d] for d in LINE_STEPS]
    places = range(PLANE - 1)
    steps = range(NZ - 1)

    for peer in line + near + [twin]:
        greet(peer)
    for c in fetch([(ept_h, ept), (query_h, query), (own_h, own), (ebt_h, ebt_a)], loads):
        c.wait()
    kept = []

    def relation_first(ids, dq, mark):
        kept.append([(ebt_a[...], dq_a[...], meta[2:3, :]), (ebt[...], dq, ids)])
        kept.append(mark + mark_a[...])
        relation_part(other, *kept, csend)

    grad_v[...] = gradients(1, blocks, ept, own, query, meta, metap, tot, rb, rbt, relation_first)
    pl.semaphore_wait(pltpu.get_barrier_semaphore(), len(line) + len(near) + 1)

    swap = send(csend, crecv, s_core.at[0], s_core.at[1], twin)
    swap.start()
    relation_part(core, *kept, acc)
    swap.wait()
    both = acc[...] + crecv[...]
    acc[...] = both
    xsend[...] = both.astype(jnp.bfloat16).reshape(PLANE, SHARE, 16, LANES)

    xcopies = [send(xsend.at[near_plane[i]], xslot.at[i], s_xs.at[i], s_xr.at[i], near[i]) for i in places]
    for c in xcopies:
        c.start()
    acc_s, fresh = adagrad(et[...], state[...], grad_v[...])
    state_out[...] = acc_s
    et_out[...] = fresh
    for c in xcopies:
        c.wait()
    part = acc[pl.ds(plane * SHARE, SHARE)]
    for i in places:
        part = part + xslot[i].astype(jnp.float32)
    zpart[...] = part.reshape(OWNERS, 8, LANES)

    def zcopy(i, piece):
        return send(zpart.at[piece], zslot.at[i], s_zs.at[i], s_zr.at[i], line[i])

    def gcopy(i, owner):
        return send(zres.at[owner], zres.at[owner], s_gs.at[i], s_gr.at[owner], line[i])

    for i in steps:
        @pl.when(line_z[i] < OWNERS)
        def _():
            zcopy(i, line_z[i]).start()

    @pl.when(z < OWNERS)
    def _():
        for i in steps:
            zcopy(i, 0).wait_recv()
        total = zpart[z]
        for i in steps:
            total = total + zslot[i]
        zres[z] = total
        for i in steps:
            gcopy(i, z).start()

    for i in steps:
        @pl.when(line_z[i] < OWNERS)
        def _():
            zcopy(i, line_z[i]).wait_send()

    for o in range(OWNERS):
        @pl.when(z != o)
        def _():
            gcopy(0, o).wait_recv()

    whole = zres[...].reshape(SHARE, 16, LANES)
    tail = whole[SHARE - 1]
    rest = tail[0:8] - tail[0:8].astype(jnp.bfloat16).astype(jnp.float32)
    tail = jnp.concatenate([tail[0:8], jnp.where(plane == PLANE - 1, rest, tail[8:16])], axis=0)
    summed[core, plane] = whole.astype(jnp.bfloat16)
    summed[core, plane, SHARE - 1] = tail.astype(jnp.bfloat16)

    def ncopy(i, piece):
        return send(summed.at[core, piece], summed.at[core, piece], s_as.at[i], s_ar.at[i], near[i])

    def tcopy(piece, slot):
        return send(summed.at[core, piece], summed.at[core, piece], s_bs.at[slot], s_br.at[slot], twin)

    for i in places:
        ncopy(i, plane).start()
    tcopy(plane, PLANE - 1).start()

    @pl.when(z < OWNERS)
    def _():
        for i in steps:
            gcopy(i, z).wait_send()

    for i in reversed(places):
        ncopy(i, from_plane[i]).wait_recv()
        tcopy(from_plane[i], i).start()
    for i in places:
        ncopy(i, plane).wait_send()

    def arrived(piece, slot):
        return send(summed.at[other, piece], summed.at[other, piece], s_bs.at[slot], s_br.at[slot], twin)

    for i in reversed(places):
        tcopy(from_plane[i], i).wait_send()
        arrived(from_plane[i], i).wait_recv()
    tcopy(plane, PLANE - 1).wait_send()
    arrived(plane, PLANE - 1).wait_recv()


def finish_kernel(et, summed, relations, tot, state, et_out, rel_out, loss_out, state_out, rel_v, out_v, sems):
    kinds, width = relations.shape[:2]
    full, tall = width // LANES, width // 16
    edge = full * LANES
    table = pltpu.make_async_copy(et, et_out, sems.at[0])
    table.start()
    loads = [pltpu.make_async_copy(relations.at[k], rel_v.at[k], sems.at[1 + k]) for k in range(kinds)]
    stores = [pltpu.make_async_copy(out_v.at[k], rel_out.at[k], sems.at[1 + kinds + k]) for k in range(kinds)]
    for c in loads:
        c.start()
    state_out[...] = state[...]
    tile = summed[0, PLANE - 1, SHARE - 1].astype(jnp.float32)
    sums = tile[0:1] + tile[8:9]
    for rnd in range(ROUNDS):
        span = slice(rnd, rnd + 1)
        loss_out[:, span] = sums[:, span] / tot[span, 0:1]
    for kind in range(kinds):
        loads[kind].wait()
        total = summed[kind].reshape(TILES, 16, LANES).astype(jnp.float32)
        for j in range(full):
            piece = total[j * tall : (j + 1) * tall].reshape(width, LANES)
            span = slice(j * LANES, (j + 1) * LANES)
            out_v[kind, :, span] = rel_v[kind, :, span] - REL_RATE * piece
        side = jnp.concatenate([total[full * tall + j] for j in range(4)], axis=1)
        out_v[kind, :, edge:] = rel_v[kind, :, edge:] - REL_RATE * side.T[:width, :]
        stores[kind].start()
    for c in stores:
        c.wait()
    table.wait()


def on_device(tables, state, relations, partner, counts, positive, relation_ids):
    rows, width = tables.shape
    blocks = lax.axis_size("blk")
    depth = blocks.bit_length() - 1
    me = lax.axis_index("blk")
    f32, bf16, i32 = jnp.float32, jnp.bfloat16, jnp.int32
    shape = jax.ShapeDtypeStruct
    DMA = pltpu.SemaphoreType.DMA
    block_f, block_b, flat_b = shape((width, rows), f32), shape((width, rows), bf16), shape((rows, width), bf16)
    ops_b, small_i, tile_f = shape(relations.shape, bf16), shape((8, rows), i32), shape((8, LANES), f32)
    accum_f, mark_f = shape((1, rows), f32), shape((16, LANES), f32)
    partial = functools.partial

    def level(rnd):
        offset = jnp.bitwise_xor(partner[rnd, 0], me)
        return sum((offset >> bit > 0).astype(i32) for bit in range(1, depth))

    def first(bit, *args):
        return pl.pallas_call(
            partial(exchange_first, bit),
            out_shape=(block_b, ops_b, ops_b, small_i, block_b, small_i, tile_f, flat_b, block_b),
            in_specs=[ANY, ANY, VMEM, VMEM, VMEM],
            out_specs=(ANY, VMEM, VMEM, VMEM, ANY, VMEM, VMEM, ANY, ANY),
            scratch_shapes=[
                pltpu.VMEM((width, rows), bf16),
                pltpu.VMEM((rows, width), bf16),
                pltpu.VMEM((width, rows), bf16),
                DMA((3,)),
                pltpu.VMEM((width, rows), f32),
                pltpu.VMEM(relations.shape, f32),
                pltpu.VMEM((8, LANES), f32),
                pltpu.VMEM((8, LANES), f32),
                pltpu.VMEM((2 * PLANE - 1, 8, LANES), f32),
                pltpu.VMEM((2 * REACH, 8, LANES), f32),
                pltpu.VMEM((2, 8, LANES), f32),
                pltpu.VMEM((2, 8, LANES), f32),
                DMA((2,)),
                DMA((4,)),
                DMA((2 * PLANE - 1,)), DMA((2 * PLANE - 1,)),
                DMA((2 * REACH,)), DMA((2 * REACH,)),
                DMA((2,)), DMA((2,)),
            ],
            compiler_params=pltpu.CompilerParams(collective_id=bit, has_side_effects=True, vmem_limit_bytes=GRANT),
            name="swap_a",
        )(*args)

    def following(bit, *args):
        return pl.pallas_call(
            partial(exchange_next, bit),
            out_shape=(block_b, small_i, flat_b, block_b),
            in_specs=[VMEM] * 3,
            out_specs=(ANY, VMEM, ANY, ANY),
            scratch_shapes=[
                pltpu.VMEM((rows, width), bf16),
                pltpu.VMEM((width, rows), bf16),
                DMA((2,)),
                DMA((4,)),
            ],
            compiler_params=pltpu.CompilerParams(collective_id=depth + bit, has_side_effects=True, vmem_limit_bytes=GRANT),
            name="swap_b",
        )(*args)

    et = tables.T
    accum = state.reshape(1, rows)
    ebt, rb, rbt, meta, ept, metap, tot, own, query = lax.switch(
        level(0), [partial(first, bit) for bit in range(depth)],
        et, relations, positive, relation_ids, counts.T)
    et, ebt2, accum, dq, mark = pl.pallas_call(
        partial(round_kernel, float(blocks)),
        out_shape=(block_f, block_b, accum_f, block_b, mark_f),
        in_specs=[ANY] * 4 + [VMEM] * 6,
        out_specs=(VMEM,) * 5,
        scratch_shapes=[
            pltpu.VMEM((width, rows), bf16),
            pltpu.VMEM((rows, width), bf16),
            pltpu.VMEM((width, rows), bf16),
            pltpu.VMEM((width, rows), f32),
            DMA((4,)),
        ],
        compiler_params=pltpu.CompilerParams(vmem_limit_bytes=GRANT),
        name="round_a",
    )(et, ept, own, query, meta, metap, tot, accum, rb, rbt)

    ept, metap, own, query = lax.switch(
        level(1), [partial(following, bit) for bit in range(depth)],
        ebt2, meta, rbt)
    et, accum_v, summed = pl.pallas_call(
        partial(last_kernel, float(blocks)),
        out_shape=(block_f, accum_f, shape((2, PLANE, SHARE, 16, LANES), bf16)),
        in_specs=[VMEM] * 2 + [ANY] * 3 + [VMEM] * 6 + [ANY] + [VMEM] * 2,
        out_specs=(VMEM,) * 3,
        scratch_shapes=[
            pltpu.VMEM((width, rows), bf16),
            pltpu.VMEM((rows, width), bf16),
            pltpu.VMEM((width, rows), bf16),
            pltpu.VMEM((width, rows), bf16),
            DMA((4,)),
            pltpu.VMEM((width, rows), f32),
            pltpu.VMEM((TILES, 16, LANES), f32),
            pltpu.VMEM((TILES, 16, LANES), f32),
            pltpu.VMEM((TILES, 16, LANES), f32),
            pltpu.VMEM((PLANE, SHARE, 16, LANES), bf16),
            pltpu.VMEM((PLANE - 1, SHARE, 16, LANES), bf16),
            pltpu.VMEM((OWNERS, 8, LANES), f32),
            pltpu.VMEM((NZ - 1, 8, LANES), f32),
            pltpu.VMEM((OWNERS, 8, LANES), f32),
            DMA((2,)),
            DMA((PLANE - 1,)), DMA((PLANE - 1,)),
            DMA((NZ - 1,)), DMA((NZ - 1,)),
            DMA((NZ - 1,)), DMA((OWNERS,)),
            DMA((PLANE - 1,)), DMA((PLANE - 1,)),
            DMA((PLANE,)), DMA((PLANE,)),
        ],
        compiler_params=pltpu.CompilerParams(collective_id=2 * depth, has_side_effects=True, vmem_limit_bytes=GRANT),
        name="last",
    )(et, ebt2, ept, own, query, meta, metap, tot, accum, rb, rbt, ebt, dq, mark)
    et, relations_out, losses, accum = pl.pallas_call(
        finish_kernel,
        out_shape=(block_f, shape(relations.shape, f32), shape((1, ROUNDS), f32), accum_f),
        in_specs=[ANY, VMEM, ANY, VMEM, VMEM],
        out_specs=(ANY, ANY, VMEM, VMEM),
        scratch_shapes=[
            pltpu.VMEM(relations.shape, f32), pltpu.VMEM(relations.shape, f32), DMA((5,)),
        ],
        compiler_params=pltpu.CompilerParams(vmem_limit_bytes=GRANT),
        name="finish",
    )(et, summed, relations, tot, accum_v)
    return (et.T, accum.reshape(rows), relations_out, losses.reshape(ROUNDS))


def solution(mesh):
    return jax.shard_map(
        on_device,
        mesh=mesh,
        in_specs=(
            P("blk", None),
            P("blk"),
            P(),
            P(None, "blk"),
            P(None, "blk"),
            P(None, "blk"),
            P(None, "blk"),
        ),
        out_specs=(P("blk", None), P("blk"), P(), P()),
        check_vma=False,
    )
```
